32 devices in a mesh: grp: 2 (over x), seq: 8 (over z, y), pool: 2 (over core).
Axes of the slice: x: 2, y: 2, z: 4, core: 2. Of those that a mesh axis runs over, the one named last changes fastest.
Arguments:
- factors: bfloat16 [2, 65536, 160], P('grp', 'seq'), parts along dimension 0, may hold values from -6 to 6
- basis: bfloat16 [2, 160, 1024], P('grp', None, 'pool'), parts along dimension 0, may hold values from -1 to 1
- value_pool: bfloat16 [2, 65536, 1024], P('grp', ('seq', 'pool')), parts along dimension 0, may hold values from -6 to 6
- page_summary: bfloat16 [2, 8192, 1024], P('grp', 'seq', 'pool'), parts along dimension 0, may hold values from -6 to 6
- recent_keys: bfloat16 [2, 64, 1024], P('grp', None, 'pool'), parts along dimension 0, may hold values from -20 to 20
- recent_values: bfloat16 [2, 64, 1024], P('grp', None, 'pool'), parts along dimension 0, may hold values from -6 to 6
- query: bfloat16 [2, 8192], P('grp', 'pool'), parts along dimension 0, may hold values from -8192 to 8192
- selected: int32 [2, 8, 1024], P('grp'), parts along dimension 0, may hold values from 0 to 8191, as said below
- owner_map: int32 [2, 8192], P('grp', 'seq'), parts along dimension 0, may hold values from 0 to 1, as said below
- lengths: int32 [2], P('grp'), parts along dimension 0, may hold values from 32768 to 65536, as said below
Outputs:
- attn: bfloat16 [2, 8192], P('grp', 'pool'), parts along dimension 0
The draws below stay inside these ranges and needn't reach their ends.
There are 2 independent parts, one for each index of `grp`. The reference program is written for one: setup_inputs(seed, part) draws one part's arguments, and reference() takes and returns one part's arrays. A program takes and returns all parts, laid end to end along the dimension named above; each array names one. Nothing has to cross between parts.
Inputs may be any that keep to these rules, and one draw needn't show every extreme that they name: `selected`: for every request and key-value head, 1024 distinct page ids in ascending order, each below ceil(lengths / 8); every aligned block of 1024 pages holds at most 256 of them, and for every request and head some block holds exactly 256. `owner_map`: in every aligned block of 1024 pages of a request exactly half of the pages have owner 1. `lengths`: some request has exactly 65536 tokens.
All inputs are finite; a program needn't handle non-finite values.
Results may differ from the reference program's by a relative error of at most 0.0075.
The reference program's roundings to bfloat16 on the way count: a program that leaves them out, or rounds other values in their place, can miss the bound.
Values may be sent and summed in bfloat16 or wider, within the bound.
A program may use at most 128 MiB of HBM per device.

```python
import math
import jax
import jax.numpy as jnp
import numpy as np
from jax import lax

HD = 128
KVH = 8
QH = 64
RANK = 160
PAGE = 8
SEL = 1024
WIN = 64
REQ = 1
L_CTX = 65536
GQA = 8
NPAGE = 8192
PAGES_DEV = 1024
MAX_PICKED_PAGES = 256
N_SEQ = 8


def length_helper(key):
    first_key, second_key = jax.random.split(jax.random.fold_in(key, 11))
    drawn_len = jax.random.randint(first_key, (REQ,), L_CTX // 2, L_CTX + 1)
    full_request = jax.random.randint(second_key, (), 0, REQ)
    return jnp.where(jnp.arange(REQ) == full_request, L_CTX, drawn_len).astype(jnp.int32)


def draw_lengths(key, part):
    return length_helper(key)


def pick_pages(key, page_count):
    count_of_blocks = NPAGE // PAGES_DEV
    first_key, second_key, key_third_part = jax.random.split(key, 3)
    local_ids = jnp.arange(PAGES_DEV, dtype=jnp.int32)
    page_ids = jnp.arange(NPAGE, dtype=jnp.int32).reshape(count_of_blocks, PAGES_DEV)
    first_score = jax.random.randint(first_key, (count_of_blocks, PAGES_DEV), 0, 32768) * PAGES_DEV + local_ids[None, :]
    first_score = jnp.where(page_ids < page_count, first_score, -1)
    cand_score, cand_local = lax.top_k(first_score, MAX_PICKED_PAGES)
    cand_page = jnp.arange(count_of_blocks, dtype=jnp.int32)[:, None] * PAGES_DEV + cand_local
    busiest_block = jax.random.randint(second_key, (), 0, count_of_blocks // 2)
    flattened_indices = jnp.arange(count_of_blocks * MAX_PICKED_PAGES, dtype=jnp.int32).reshape(count_of_blocks, MAX_PICKED_PAGES)
    extra_credit = jnp.where(jnp.arange(count_of_blocks)[:, None] == busiest_block, 2 ** 30, 0)
    runner_up_score = jax.random.randint(key_third_part, (count_of_blocks, MAX_PICKED_PAGES), 0, 32768) * (count_of_blocks * MAX_PICKED_PAGES) + flattened_indices + extra_credit
    runner_up_score = jnp.where(cand_score >= 0, runner_up_score, -1)
    unused, chosen = lax.top_k(runner_up_score.reshape(-1), SEL)
    pages = cand_page.reshape(-1)[chosen]
    return jnp.sort(pages).astype(jnp.int32)


def selected_pages(key):
    lengths = length_helper(key)
    page_count = (lengths + PAGE - 1) // PAGE
    counts_rep = jnp.repeat(page_count, KVH)
    subkeys = jax.random.split(jax.random.fold_in(key, 23), REQ * KVH)
    pages = jax.vmap(pick_pages)(subkeys, counts_rep)
    return pages.reshape(REQ, KVH, SEL)


def draw_selected(key, part):
    return selected_pages(key)


def draw_owner_map(key, part):
    count_of_blocks = NPAGE // PAGES_DEV
    subkeys = jax.random.split(jax.random.fold_in(key, 5), REQ * count_of_blocks)
    permuted = jax.vmap(lambda sub_key: jax.random.permutation(sub_key, PAGES_DEV))(subkeys)
    return (permuted < PAGES_DEV // 2).astype(jnp.int32).reshape(REQ, NPAGE)


def factor_values(key):
    return jax.random.truncated_normal(jax.random.fold_in(key, 61), -6.0, 6.0, (REQ, L_CTX, RANK), jnp.float32)


def basis_values(key):
    return jax.random.truncated_normal(jax.random.fold_in(key, 67), -3.0, 3.0, (REQ, RANK, KVH * HD), jnp.float32) * RANK ** (-0.5)


def draw_factors(key, part):
    return factor_values(key).astype(jnp.bfloat16)


def draw_basis(key, part):
    return basis_values(key).astype(jnp.bfloat16)


def base_draw(key):
    query_key, recent_key = jax.random.split(jax.random.fold_in(key, 41), 2)
    base_query = jax.random.truncated_normal(query_key, -6.0, 6.0, (REQ, KVH, GQA, HD), jnp.float32)
    mean_query = jnp.mean(base_query, axis=2)
    recent_set = jax.random.truncated_normal(recent_key, -6.0, 6.0, (REQ, WIN, KVH, HD), jnp.float32) + 2.0 * mean_query[:, None]
    return (base_query, recent_set)


def draw_query(key, part):
    base_query, recent_set = base_draw(key)
    return base_query.reshape(REQ, QH * HD).astype(jnp.bfloat16)


def draw_recent_keys(key, part):
    base_query, recent_set = base_draw(key)
    return recent_set.reshape(REQ, WIN, KVH * HD).astype(jnp.bfloat16)


def block_levels(rng, extent, shards, least, top_value):
    def one(dim, shards_of):
        heights = jax.random.uniform(jax.random.fold_in(jax.random.fold_in(rng, 6), dim), (shards_of,), jnp.float32, least / len(shards), top_value / len(shards))
        return jnp.repeat(jnp.exp(heights), extent[dim] // shards_of).reshape((-1,) + (1,) * (len(extent) - dim - 1))

    factor_of = one(*shards[0])
    for cut in shards[1:]:
        factor_of = factor_of * one(*cut)
    return factor_of


def bell_draw(own_key, dims, spread, limit, pieces=(), kind=jnp.bfloat16):
    entries = jax.random.normal(own_key, dims, jnp.float32) * spread
    if len(pieces) > 0:
        entries = block_levels(own_key, dims, pieces, -0.22, 0.18) * entries
    return jnp.clip(entries, min=-limit, max=limit).astype(kind)


def setup_inputs(seed: int = 0, part: int = 0) -> dict:
    key_list = jax.random.split(jax.random.key(seed), 11)
    own_keys = jax.random.split(jax.random.fold_in(key_list[10], part), 11)
    factors = draw_factors(jax.random.fold_in(jax.random.fold_in(key_list[10], part), 71), part)
    basis = draw_basis(jax.random.fold_in(jax.random.fold_in(key_list[10], part), 71), part)
    value_pool = bell_draw(own_keys[2], (REQ, L_CTX, KVH * HD), 1.0, 6.0, ((1, 16),))
    page_summary = bell_draw(own_keys[3], (REQ, NPAGE, KVH * HD), 1.0, 6.0, ((1, 8), (2, 2)))
    recent_keys = draw_recent_keys(jax.random.fold_in(jax.random.fold_in(key_list[10], part), 71), part)
    recent_values = bell_draw(own_keys[5], (REQ, WIN, KVH * HD), 1.0, 6.0, ((2, 2),))
    query = draw_query(jax.random.fold_in(jax.random.fold_in(key_list[10], part), 71), part)
    selected = draw_selected(jax.random.fold_in(jax.random.fold_in(key_list[10], part), 71), part)
    owner_map = draw_owner_map(jax.random.fold_in(jax.random.fold_in(key_list[10], part), 71), part)
    lengths = draw_lengths(jax.random.fold_in(jax.random.fold_in(key_list[10], part), 71), part)
    return dict(factors=factors, basis=basis, value_pool=value_pool, page_summary=page_summary, recent_keys=recent_keys, recent_values=recent_values, query=query, selected=selected, owner_map=owner_map, lengths=lengths)


def llama_rates(head_dim):
    half_dim = head_dim // 2
    base_rates = 500000.0 ** (-(np.arange(half_dim) * 2.0) / head_dim)
    wavelen = 2.0 * math.pi / base_rates
    smooth = (8192.0 / wavelen - 1.0) / 3.0
    blended = (1.0 - smooth) * base_rates / 8.0 + smooth * base_rates
    return np.where(wavelen < 2048.0, base_rates, np.where(wavelen > 8192.0, base_rates / 8.0, blended))


def angle_tables(length, head_dim):
    inv_rates = llama_rates(head_dim)
    coarse = (np.arange(length // 256) * 256.0)[:, None] * inv_rates[None, :]
    fine_angles = (np.arange(256) * 1.0)[:, None] * inv_rates[None, :]
    return np.cos(coarse), np.sin(coarse), np.cos(fine_angles), np.sin(fine_angles)


def combine_angles(coarse_cos, coarse_sin, fine_cos, fine_sin):
    cosine = coarse_cos[:, None, :] * fine_cos[None, :, :] - coarse_sin[:, None, :] * fine_sin[None, :, :]
    sine_table = coarse_sin[:, None, :] * fine_cos[None, :, :] + coarse_cos[:, None, :] * fine_sin[None, :, :]
    row_count = coarse_cos.shape[0] * 256
    return cosine.reshape(row_count, -1), sine_table.reshape(row_count, -1)


def rotate(values, cosine, sine_table):
    half_dim = values.shape[-1] // 2
    first_half = values[..., :half_dim]
    second_half = values[..., half_dim:]
    return jnp.concatenate([first_half * cosine - second_half * sine_table, second_half * cosine + first_half * sine_table], axis=-1)


def reference(factors, basis, value_pool, page_summary, recent_keys, recent_values, query, selected, owner_map, lengths):
    tables = angle_tables(L_CTX, HD)
    cosine, sine_table = combine_angles(*[jnp.asarray(table, jnp.float32) for table in tables])
    positions = jnp.arange(L_CTX, dtype=jnp.int32)
    score_scale = HD ** -0.5
    block_pages = NPAGE // N_SEQ
    outputs = []
    for request in range(REQ):
        owners = owner_map[request].reshape(N_SEQ, block_pages)
        ones_count = jnp.cumsum(owners, axis=1).astype(jnp.int32)
        zeros_count = jnp.cumsum(1 - owners, axis=1).astype(jnp.int32)
        page_rank = jnp.where(owners == 1, ones_count, zeros_count) - 1
        page_slot = (jnp.arange(N_SEQ, dtype=jnp.int32)[:, None] * block_pages + owners * (block_pages // 2) + page_rank).reshape(NPAGE).astype(jnp.int32)
        in_range = positions < lengths[request]
        page_valid = in_range.reshape(NPAGE, PAGE)
        any_valid = jnp.any(page_valid, axis=1)

        def one_head(head_id):
            columns = lax.dynamic_slice_in_dim(basis[request], head_id * HD, HD, 1)
            stacked = jnp.dot(factors[request], columns, preferred_element_type=jnp.float32)
            keys_bf = rotate(stacked, cosine, sine_table).astype(jnp.bfloat16)
            paged_keys = keys_bf.reshape(NPAGE, PAGE, HD)
            low_keys = jnp.min(jnp.where(page_valid[:, :, None], paged_keys, jnp.inf), axis=1)
            high_keys = jnp.max(jnp.where(page_valid[:, :, None], paged_keys, -jnp.inf), axis=1)
            center = jnp.where(any_valid[:, None], (low_keys.astype(jnp.float32) + high_keys.astype(jnp.float32)) * 0.5, 0.0).astype(jnp.bfloat16)
            chosen = selected[request, head_id]
            picked_mask = jnp.zeros((NPAGE,), jnp.int32).at[chosen].set(1)
            q_rows = lax.dynamic_slice_in_dim(query[request], head_id * GQA * HD, GQA * HD, 0).reshape(GQA, HD)
            land_scores = jnp.dot(q_rows, center.T, preferred_element_type=jnp.float32) * score_scale
            land_scores = jnp.where((any_valid & (picked_mask == 0))[None, :], land_scores, -jnp.inf)
            tokens = (chosen[:, None] * PAGE + jnp.arange(PAGE, dtype=jnp.int32)[None, :]).reshape(SEL * PAGE)
            exact_scores = jnp.dot(q_rows, keys_bf[tokens].T, preferred_element_type=jnp.float32) * score_scale
            exact_scores = jnp.where(in_range[tokens][None, :], exact_scores, -jnp.inf)
            value_rows = (page_slot[chosen][:, None] * PAGE + jnp.arange(PAGE, dtype=jnp.int32)[None, :]).reshape(SEL * PAGE)
            head_values = lax.dynamic_slice_in_dim(value_pool[request], head_id * HD, HD, 1)
            exact_values = head_values[value_rows]
            land_values = lax.dynamic_slice_in_dim(page_summary[request], head_id * HD, HD, 1)
            recent_k = lax.dynamic_slice_in_dim(recent_keys[request], head_id * HD, HD, 1)
            recent_v = lax.dynamic_slice_in_dim(recent_values[request], head_id * HD, HD, 1)
            recent_scores = jnp.dot(q_rows, recent_k.T, preferred_element_type=jnp.float32) * score_scale
            scores = jnp.concatenate([exact_scores, land_scores, recent_scores], axis=1)
            all_values = jnp.concatenate([exact_values, land_values, recent_v], axis=0)
            row_peak = jnp.max(scores, axis=1, keepdims=True)
            weights = jnp.exp(scores - row_peak)
            weight_sum = jnp.sum(weights, axis=1, keepdims=True)
            mixed_out = jnp.dot(weights.astype(jnp.bfloat16), all_values, preferred_element_type=jnp.float32) / weight_sum
            return mixed_out.astype(jnp.bfloat16)

        per_head = lax.map(one_head, jnp.arange(KVH, dtype=jnp.int32))
        outputs.append(per_head.reshape(QH * HD))
    return jnp.stack(outputs)
```

```python
import functools
import math

import jax
import jax.numpy as jnp
import numpy as np
from jax import lax
from jax.experimental import pallas as pl
from jax.experimental.pallas import tpu as pltpu
from jax.sharding import PartitionSpec as P

HD = 128
PAGE = 8
WIN = 64
LANES = 128
FINE = 256
HALF = HD // 2
GROUP = FINE // PAGE
MESH = pl.DeviceIdType.MESH
BF = jnp.bfloat16
F32 = jnp.float32


def llama_rates(head_dim):
    half_dim = head_dim // 2
    base_rates = 500000.0 ** (-(np.arange(half_dim) * 2.0) / head_dim)
    wavelen = 2.0 * math.pi / base_rates
    smooth = (8192.0 / wavelen - 1.0) / 3.0
    blended = (1.0 - smooth) * base_rates / 8.0 + smooth * base_rates
    return np.where(
        wavelen < 2048.0, base_rates, np.where(wavelen > 8192.0, base_rates / 8.0, blended)
    )


def angle_tables(length, seq_count):
    rates = llama_rates(HD)

    def pair(angles):
        return [np.concatenate([f(angles)] * 2, axis=1) for f in (np.cos, np.sin)]

    coarse = pair((np.arange(length // FINE) * float(FINE))[:, None] * rates[None, :])
    coarse = np.stack([t.reshape(seq_count, -1, HD) for t in coarse], axis=1)
    middle = pair((np.arange(GROUP) * float(PAGE) + (PAGE - 1) * 0.5)[:, None] * rates[None, :])
    inner = pair((np.arange(PAGE // 2) + 0.5)[:, None] * rates[None, :])
    return coarse.astype(np.float32), np.concatenate(middle + inner, axis=0).astype(np.float32)


def nt(a, b):
    return lax.dot_general(a, b, (((1,), (1,)), ((), ())), preferred_element_type=F32)


def tn(a, b):
    return lax.dot_general(a, b, (((0,), (0,)), ((), ())), preferred_element_type=F32)


def nn(a, b):
    return jnp.dot(a, b, preferred_element_type=F32)


def ones_where(mask):
    return jnp.where(mask, 1.0, 0.0).astype(BF)


def iota(shape, dim):
    return lax.broadcasted_iota(jnp.int32, shape, dim)


def half_swap(x):
    return pltpu.roll(x, HALF, axis=1)


def attention_kernel(
    heads,
    seq_count,
    len_ref,
    q_ref,
    sel_ref,
    own_ref,
    fine_ref,
    coarse_hbm,
    basis_hbm,
    rk_hbm,
    rv_hbm,
    fac_hbm,
    sum_hbm,
    pool_hbm,
    out_ref,
    coarse,
    basis_in,
    recent_keys,
    recent_values,
    fac,
    summary,
    values,
    basis,
    halves,
    keys,
    centers,
    live,
    scores,
    land,
    wbuf,
    onehot,
    outgoing,
    own_w,
    theirs,
    other_out,
    bodies,
    stats,
    f_sem,
    i_sem,
    v_sem,
    pair_sem,
    send_sem,
    recv_sem,
):
    seq_pos = lax.axis_index("seq")
    core = lax.axis_index("pool")
    rows = q_ref.shape[1] // HD
    gqa = rows // heads
    pairs = heads // 2
    width = heads * HD
    tokens = fac.shape[1]
    pages = tokens // PAGE
    chunks = pages // LANES
    span = LANES * PAGE
    parts = values.shape[0] // span
    limit = len_ref[0] - seq_pos * tokens
    scale = HD ** (-0.5) * math.log2(math.e)
    partner = {"pool": 1 - core}

    def fac_load(n):
        at = pl.ds(n * span, span)
        return pltpu.make_async_copy(fac_hbm.at[:, at], fac.at[:, at], f_sem.at[n])

    def load(src, dst, n):
        copy = pltpu.make_async_copy(src, dst, i_sem.at[n])
        copy.start()
        return copy

    fac_loads = [fac_load(n) for n in range(chunks)]
    basis_load = load(basis_hbm, basis_in, 0)
    fac_loads[0].start()
    coarse_load = load(coarse_hbm.at[seq_pos], coarse, 1)
    for n in range(1, chunks):
        fac_loads[n].start()
    rk_load = load(rk_hbm, recent_keys, 2)
    rv_load = load(rv_hbm, recent_values, 3)
    sum_load = load(sum_hbm, summary, 4)
    loads = []
    for g in range(parts):
        at = pl.ds(g * span, span)
        copy = pltpu.make_async_copy(pool_hbm.at[at, :], values.at[at, :], v_sem.at[g])
        copy.start()
        loads.append(copy)

    barrier = pltpu.get_barrier_semaphore()
    for k in range(seq_count):
        peer = lax.rem(seq_pos + k, seq_count)
        for pool in (core, 1 - core)[k == 0 :]:
            pl.semaphore_signal(
                barrier,
                inc=1,
                device_id={"seq": peer, "pool": pool},
                device_id_type=MESH,
            )

    low_half = iota((1, LANES), 1) < HALF
    q_flat = q_ref[...].astype(F32)
    q_rows = jnp.concatenate([q_flat[:, r * HD : (r + 1) * HD] for r in range(rows)], axis=0)
    q_swap = half_swap(q_rows)
    q_pairs = []
    q_plain = []
    for p in range(pairs):
        first = slice(2 * p * gqa, (2 * p + 1) * gqa)
        second = slice((2 * p + 1) * gqa, (2 * p + 2) * gqa)
        x = jnp.concatenate(
            [jnp.where(low_half, q_rows[first], 0.0), jnp.where(low_half, 0.0, q_swap[second])], axis=0
        )
        y = jnp.concatenate(
            [jnp.where(low_half, q_swap[first], 0.0), jnp.where(low_half, 0.0, q_rows[second])], axis=0
        )
        q_pairs.append(jnp.concatenate([x, y], axis=1).astype(BF))
        zero = jnp.zeros((gqa, HD), F32)
        plain = [
            jnp.concatenate([q_rows[first], zero], axis=1),
            jnp.concatenate([zero, q_rows[second]], axis=1),
        ]
        q_plain.append(jnp.concatenate(plain, axis=0).astype(BF))

    sel = jnp.where(core == 0, sel_ref[:heads, :], sel_ref[heads:, :]) - seq_pos * pages
    count = sel.shape[1]
    page_tok = iota((1, pages), 1) * PAGE
    for h in range(heads):
        ids = sel[h : h + 1, :]
        hi = jnp.floor_divide(ids, LANES)
        lo = ids - hi * LANES
        hit = nt(
            ones_where(iota((8, count), 0) == hi), ones_where(iota((LANES, count), 0) == lo)
        )
        row = jnp.concatenate([hit[c : c + 1, :] for c in range(chunks)], axis=1)
        left = jnp.where(row > 0.5, limit - page_tok, 0)
        live[h * gqa : (h + 1) * gqa, :] = jnp.broadcast_to(left, (gqa, pages))

    owners = own_ref[...]
    before = nn(
        ones_where(owners == 1), ones_where(iota((LANES, LANES), 0) < iota((LANES, LANES), 1))
    )
    chunk_total = jnp.sum(owners.astype(F32), axis=1, keepdims=True)
    running = jnp.zeros((1, 1), F32)
    slots = []
    for c in range(chunks):
        ones = before[c : c + 1, :] + running
        running = running + chunk_total[c : c + 1, :]
        page = (iota((1, LANES), 1) + c * LANES).astype(F32)
        slots.append(jnp.where(owners[c : c + 1, :] == 1, ones + pages // 2, page - ones))
    slot = jnp.concatenate(slots, axis=1).astype(jnp.int32)
    slot = slot - (1 - core) * (pages // 2)
    slot = jnp.where(slot < 0, slot + pages, slot)
    place = slot % LANES
    column = slot - place + place % 16 * PAGE + place // 16
    for c in range(chunks):
        onehot[c * LANES : (c + 1) * LANES, :] = ones_where(
            iota((LANES, pages), 0) == column - c * LANES
        )

    basis_load.wait()
    for p in range(pairs):
        a = basis_in[:, 2 * p * HD : (2 * p + 1) * HD].astype(F32)
        b = basis_in[:, (2 * p + 1) * HD : (2 * p + 2) * HD].astype(F32)
        basis[:, 2 * p * HD : (2 * p + 1) * HD] = jnp.where(low_half, a, half_swap(b)).astype(BF)
        basis[:, (2 * p + 1) * HD : (2 * p + 2) * HD] = jnp.where(low_half, half_swap(a), b).astype(BF)

    def multiply(n):
        for k in range(span // FINE):
            at = n * span + k * FINE
            u = tn(fac[:, at : at + FINE], basis[...])
            for c in range(heads):
                halves[n % 2, c, k * FINE : (k + 1) * FINE, :] = u[:, c * HD : (c + 1) * HD]

    def rotate(n):
        for g in range(LANES // 16):
            j = n * (span // FINE) + g // 2
            cj, sj = coarse[0, j : j + 1, :], coarse[1, j : j + 1, :]
            at = g % 2 * 16
            cm = fine_ref[at : at + 16, :]
            sm = fine_ref[GROUP + at : GROUP + at + 16, :]
            ca = cj * cm - sj * sm
            sa = sj * cm + cj * sm
            low = [None] * heads
            high = [None] * heads
            for k in range(PAGE // 2):
                cb = fine_ref[2 * GROUP + k : 2 * GROUP + k + 1, :]
                sb = fine_ref[2 * GROUP + PAGE // 2 + k : 2 * GROUP + PAGE // 2 + k + 1, :]
                cc, ss, sc, cs = ca * cb, sa * sb, sa * cb, ca * sb
                for i, cosine, sine in (
                    (PAGE // 2 - 1 - k, cc + ss, sc - cs),
                    (PAGE // 2 + k, cc - ss, sc + cs),
                ):
                    row = n * span + i * LANES + g * 16
                    for p in range(pairs):
                        here = pl.ds(g * 16 * PAGE + i, 16, stride=PAGE)
                        x = halves[n % 2, 2 * p, here, :]
                        y = halves[n % 2, 2 * p + 1, here, :]
                        for c, val in (
                            (2 * p, x * cosine - y * sine),
                            (2 * p + 1, y * cosine + x * sine),
                        ):
                            key = val.astype(BF)
                            keys[row : row + 16, c * HD : (c + 1) * HD] = key
                            low[c] = key if low[c] is None else jnp.minimum(low[c], key)
                            high[c] = key if high[c] is None else jnp.maximum(high[c], key)
            row = n * LANES + g * 16
            for c in range(heads):
                centers[row : row + 16, c * HD : (c + 1) * HD] = low[c] + high[c]

    def score(n, tops):
        tops = list(tops)
        for k in range(span // FINE):
            at = n * span + k * FINE
            for p in range(pairs):
                mine = slice(p * 2 * gqa, (p + 1) * 2 * gqa)
                s = nt(q_pairs[p], keys[at : at + FINE, p * 2 * HD : (p + 1) * 2 * HD]) * scale
                left = live[mine, n * LANES : (n + 1) * LANES]
                for e in range(FINE // LANES):
                    i = k * (FINE // LANES) + e
                    one = jnp.where(left > i, s[:, e * LANES : (e + 1) * LANES], -jnp.inf)
                    scores[n, mine, i * LANES : (i + 1) * LANES] = one
                    tops[p] = jnp.maximum(tops[p], one)
        return tops

    coarse_load.wait()
    tops = [jnp.full((2 * gqa, LANES), -1e30, F32)] * pairs
    fac_loads[0].wait()
    multiply(0)
    for n in range(chunks):
        if n + 1 < chunks:
            fac_loads[n + 1].wait()
            multiply(n + 1)
        rotate(n)
        tops = score(n, tops)

    rk_load.wait()
    peaks = []
    recents = []
    for p in range(pairs):
        mine = slice(p * 2 * gqa, (p + 1) * 2 * gqa)
        cols = slice(p * 2 * HD, (p + 1) * 2 * HD)
        s = nt(q_pairs[p], centers[:, cols]) * (scale * 0.5)
        s = jnp.where((page_tok < limit) & (live[mine, :] <= 0), s, -jnp.inf)
        land[mine, :] = s
        recent = nt(q_plain[p], recent_keys[:, cols]) * scale
        first = jnp.zeros(recent.shape, jnp.int32) + seq_pos
        recent = jnp.where(first == 0, recent, -jnp.inf)
        recents.append(recent)
        best = jnp.maximum(jnp.max(tops[p], axis=1, keepdims=True), jnp.max(s, axis=1, keepdims=True))
        peaks.append(jnp.maximum(best, jnp.max(recent, axis=1, keepdims=True)))

    totals = [jnp.zeros((2 * gqa, LANES), F32)] * pairs
    for n in range(chunks):
        for p in range(pairs):
            mine = slice(p * 2 * gqa, (p + 1) * 2 * gqa)
            for i in range(PAGE):
                w = jnp.exp2(scores[n, mine, i * LANES : (i + 1) * LANES] - peaks[p])
                totals[p] = totals[p] + w
                row = i * rows + p * 2 * gqa
                wbuf[row : row + 2 * gqa, n * LANES : (n + 1) * LANES] = w.astype(BF)

    lane = iota((1, LANES), 1)

    def regroup(moved, ref):
        for t in range(pages // 2 // LANES):
            for b in range(rows // 16):
                parts_of = [
                    moved[i * rows + b * 16 : i * rows + b * 16 + 16, t * LANES : (t + 1) * LANES]
                    for i in range(PAGE)
                ]
                for bit in (1, 2, 4):
                    clear = lane // bit % 2 == 0
                    for i in range(PAGE):
                        if i & bit == 0:
                            a, c = parts_of[i], parts_of[i | bit]
                            parts_of[i] = jnp.where(clear, a, pltpu.roll(c, bit, axis=1))
                            parts_of[i | bit] = jnp.where(
                                clear, pltpu.roll(a, LANES - bit, axis=1), c
                            )
                for i in range(PAGE):
                    at = t * span + i * LANES
                    ref[b * 16 : (b + 1) * 16, at : at + LANES] = parts_of[i].astype(BF)

    regroup(nt(wbuf[...], onehot[0 : pages // 2, :]), outgoing)

    def copy_to(src, dst, sems, device):
        copy = pltpu.make_async_remote_copy(
            src_ref=src,
            dst_ref=dst,
            send_sem=sems[0],
            recv_sem=sems[1],
            device_id=device,
            device_id_type=MESH,
        )
        copy.start()
        return copy

    def spread(src, dst, n, pool, begin):
        return [
            copy_to(
                src,
                dst,
                (send_sem.at[n, k], recv_sem.at[n, k]),
                {"seq": lax.rem(seq_pos + k, seq_count), "pool": pool},
            )
            for k in range(begin, seq_count)
        ]

    pl.semaphore_wait(barrier, 2 * seq_count - 1)
    swap = copy_to(outgoing, theirs, (pair_sem.at[0], pair_sem.at[1]), partner)
    regroup(nt(wbuf[...], onehot[pages // 2 : pages, :]), own_w)

    at_lane = iota((rows, LANES), 0) == iota((rows, LANES), 1)
    land_w = []
    recent_w = []
    sums = []
    for p in range(pairs):
        mine = slice(p * 2 * gqa, (p + 1) * 2 * gqa)
        w = jnp.exp2(land[mine, :] - peaks[p])
        r = jnp.exp2(recents[p] - peaks[p])
        sums.append(
            jnp.sum(w, axis=1, keepdims=True)
            + jnp.sum(totals[p], axis=1, keepdims=True)
            + jnp.sum(r, axis=1, keepdims=True)
        )
        land_w.append(w.astype(BF))
        recent_w.append(r.astype(BF))
    as_rows = [
        jnp.sum(
            jnp.where(at_lane, jnp.concatenate(col_of, axis=0), 0.0), axis=0, keepdims=True
        )
        for col_of in (peaks, sums)
    ]
    stats[seq_pos] = jnp.concatenate(as_rows + [jnp.zeros((6, LANES), F32)], axis=0)
    stat_sends = spread(stats.at[seq_pos], stats.at[seq_pos], 0, core, 1)

    def diagonal(blocks):
        return jnp.concatenate(
            [
                blocks[h // 2][h % 2 * gqa : (h % 2 + 1) * gqa, h % 2 * HD : (h % 2 + 1) * HD]
                for h in range(heads)
            ],
            axis=0,
        )

    def weighted(ref, p, g, first):
        cols = pl.ds(pl.multiple_of(first + p * 2 * HD, 2 * HD), 2 * HD)
        return nn(
            ref[p * 2 * gqa : (p + 1) * 2 * gqa, g * span : (g + 1) * span],
            values[g * span : (g + 1) * span, cols],
        )

    rv_load.wait()
    sum_load.wait()
    mine = []
    for p in range(pairs):
        cols = slice(p * 2 * HD, (p + 1) * 2 * HD)
        mine.append(nn(land_w[p], summary[:, cols]) + nn(recent_w[p], recent_values[:, cols]))
    for g in range(parts):
        loads[g].wait()
        for p in range(pairs):
            mine[p] = mine[p] + weighted(own_w, p, g, core * width)
    bodies[core, seq_pos] = diagonal(mine).astype(BF)
    sends = spread(bodies.at[core, seq_pos], bodies.at[core, seq_pos], 1, core, 1)
    swap.wait()
    other = [jnp.zeros((2 * gqa, 2 * HD), F32)] * pairs
    for g in range(parts):
        for p in range(pairs):
            other[p] = other[p] + weighted(theirs, p, g, (1 - core) * width)
    other_out[...] = diagonal(other).astype(BF)
    sends = sends + spread(other_out, bodies.at[core, seq_pos], 2, 1 - core, 0)

    for send in stat_sends:
        send.wait()
    peak_rows = [stats[k, 0:1, :] for k in range(seq_count)]
    joint = functools.reduce(jnp.maximum, peak_rows)

    def column_of(row):
        return jnp.sum(jnp.where(at_lane, row, 0.0), axis=1, keepdims=True)

    weight_sum = jnp.zeros((1, LANES), F32)
    factors = []
    for k in range(seq_count):
        factor = jnp.exp2(peak_rows[k] - joint)
        weight_sum = weight_sum + stats[k, 1:2, :] * factor
        factors.append(factor)
    inverse = 1.0 / weight_sum
    factors = [column_of(factor * inverse) for factor in factors]
    for send in sends:
        send.wait()
    result = jnp.zeros((rows, LANES), F32)
    for k in range(seq_count):
        result = result + (bodies[0, k].astype(F32) + bodies[1, k].astype(F32)) * factors[k]
    out_ref[...] = jnp.concatenate([result[r : r + 1, :] for r in range(rows)], axis=1).astype(BF)


def local(
    seq_count,
    factors,
    basis,
    value_pool,
    page_summary,
    recent_keys,
    recent_values,
    query,
    selected,
    owner_map,
    lengths,
):
    tokens, rank_dim = factors.shape[1:]
    width = basis.shape[2]
    heads = width // HD
    rows = query.shape[1] // HD
    pages = tokens // PAGE
    chunks = pages // LANES
    span = LANES * PAGE
    parts = value_pool.shape[1] // span
    coarse, fine = [jnp.asarray(t) for t in angle_tables(tokens * seq_count, seq_count)]
    vmem = pl.BlockSpec(memory_space=pltpu.VMEM)
    hbm = pl.BlockSpec(memory_space=pl.ANY)
    dma = pltpu.SemaphoreType.DMA
    return pl.pallas_call(
        functools.partial(attention_kernel, heads, seq_count),
        out_shape=jax.ShapeDtypeStruct((1, rows * HD), BF),
        in_specs=[pl.BlockSpec(memory_space=pltpu.SMEM)] + [vmem] * 4 + [hbm] * 7,
        out_specs=vmem,
        scratch_shapes=[
            pltpu.VMEM(coarse.shape[1:], F32),
            pltpu.VMEM((rank_dim, width), BF),
            pltpu.VMEM((WIN, width), BF),
            pltpu.VMEM((WIN, width), BF),
            pltpu.VMEM((rank_dim, tokens), BF),
            pltpu.VMEM((pages, width), BF),
            pltpu.VMEM(value_pool.shape[1:], BF),
            pltpu.VMEM((rank_dim, width), BF),
            pltpu.VMEM((2, heads, span, HD), F32),
            pltpu.VMEM((tokens, width), BF),
            pltpu.VMEM((pages, width), BF),
            pltpu.VMEM((rows, pages), jnp.int32),
            pltpu.VMEM((chunks, rows, span), F32),
            pltpu.VMEM((rows, pages), F32),
            pltpu.VMEM((PAGE * rows, pages), BF),
            pltpu.VMEM((pages, pages), BF),
            pltpu.VMEM((rows, parts * span), BF),
            pltpu.VMEM((rows, parts * span), BF),
            pltpu.VMEM((rows, parts * span), BF),
            pltpu.VMEM((rows, LANES), BF),
            pltpu.VMEM((2, seq_count, rows, LANES), BF),
            pltpu.VMEM((seq_count, 8, LANES), F32),
            dma((chunks,)),
            dma((5,)),
            dma((parts,)),
            dma((2,)),
            dma((3, seq_count)),
            dma((3, seq_count)),
        ],
        compiler_params=pltpu.CompilerParams(
            collective_id=0, has_side_effects=True, vmem_limit_bytes=60 * 1024 * 1024
        ),
    )(
        lengths,
        query,
        selected[0],
        owner_map.reshape(chunks, LANES),
        fine,
        coarse,
        basis[0],
        recent_keys[0],
        recent_values[0],
        jnp.swapaxes(factors[0], 0, 1),
        page_summary[0],
        value_pool[0],
    )


def solution(mesh):
    placed = (
        P("grp", "seq", None),
        P("grp", None, "pool"),
        P("grp", ("seq", "pool"), None),
        P("grp", "seq", "pool"),
        P("grp", None, "pool"),
        P("grp", None, "pool"),
        P("grp", "pool"),
        P("grp", None, None),
        P("grp", "seq"),
        P("grp"),
    )
    return jax.shard_map(
        functools.partial(local, mesh.shape["seq"]),
        mesh=mesh,
        in_specs=placed,
        out_specs=P("grp", "pool"),
        check_vma=False,
    )
```

```python
import functools
import math

import jax
import jax.numpy as jnp
import numpy as np
from jax import lax
from jax.experimental import pallas as pl
from jax.experimental.pallas import tpu as pltpu
from jax.sharding import PartitionSpec as P

HD = 128
PAGE = 8
WIN = 64
LANES = 128
FINE = 256
HALF = HD // 2
SIXTEEN = 16
ORDER = (3, 4, 2, 5, 1, 6, 0, 7)
GROUP = FINE // PAGE
MESH = pl.DeviceIdType.MESH
BF = jnp.bfloat16
F32 = jnp.float32


def llama_rates(head_dim):
    half_dim = head_dim // 2
    base_rates = 500000.0 ** (-(np.arange(half_dim) * 2.0) / head_dim)
    wavelen = 2.0 * math.pi / base_rates
    smooth = (8192.0 / wavelen - 1.0) / 3.0
    blended = (1.0 - smooth) * base_rates / 8.0 + smooth * base_rates
    return np.where(
        wavelen < 2048.0, base_rates, np.where(wavelen > 8192.0, base_rates / 8.0, blended)
    )


def angle_tables(length, seq_count):
    rates = llama_rates(HD)

    def pair(angles):
        return [np.concatenate([f(angles)] * 2, axis=1) for f in (np.cos, np.sin)]

    coarse = pair((np.arange(length // FINE) * float(FINE))[:, None] * rates[None, :])
    coarse = np.stack([t.reshape(seq_count, -1, HD) for t in coarse], axis=1)
    middle = pair((np.arange(GROUP) * float(PAGE) + (PAGE - 1) * 0.5)[:, None] * rates[None, :])
    inner = pair((np.arange(PAGE // 2) + 0.5)[:, None] * rates[None, :])
    return coarse.astype(np.float32), np.concatenate(middle + inner, axis=0).astype(np.float32)


def nt(a, b):
    return lax.dot_general(a, b, (((1,), (1,)), ((), ())), preferred_element_type=F32)


def tn(a, b):
    return lax.dot_general(a, b, (((0,), (0,)), ((), ())), preferred_element_type=F32)


def nn(a, b):
    return jnp.dot(a, b, preferred_element_type=F32)


def ones_where(mask):
    return jnp.where(mask, 1.0, 0.0).astype(BF)


def iota(shape, dim):
    return lax.broadcasted_iota(jnp.int32, shape, dim)


def half_swap(x):
    return pltpu.roll(x, HALF, axis=1)


def attention_kernel(
    heads,
    seq_count,
    len_ref,
    q_hbm,
    sel_hbm,
    own_hbm,
    fine_hbm,
    coarse_hbm,
    basis_hbm,
    rk_hbm,
    rv_hbm,
    fac_hbm,
    sum_hbm,
    pool_hbm,
    out_ref,
    q_ref,
    sel_ref,
    own_ref,
    fine_ref,
    coarse,
    basis_in,
    recent_keys,
    recent_values,
    fac,
    summary,
    values,
    basis,
    centers,
    live,
    scores,
    land,
    wbuf,
    onehot,
    outgoing,
    own_w,
    theirs,
    other_out,
    bodies,
    stats,
    f_sem,
    i_sem,
    v_sem,
    pair_sem,
    send_sem,
    recv_sem,
):
    seq_pos = lax.axis_index("seq")
    core = lax.axis_index("pool")
    rows = q_ref.shape[1] // HD
    gqa = rows // heads
    pairs = heads // 2
    width = heads * HD
    tokens = fac.shape[1]
    pages = tokens // PAGE
    chunks = pages // LANES
    span = LANES * PAGE
    groups = tokens // LANES
    rank_dim = fac.shape[0]
    parts = values.shape[0] // span
    limit = len_ref[0] - seq_pos * tokens
    scale = HD ** (-0.5) * math.log2(math.e)
    partner = {"pool": 1 - core}

    def fac_load(n):
        at = pl.ds(n * span, span)
        return pltpu.make_async_copy(fac_hbm.at[:, at], fac.at[:, at], f_sem.at[n])

    def load(src, dst, n):
        copy = pltpu.make_async_copy(src, dst, i_sem.at[n])
        copy.start()
        return copy

    fac_loads = [fac_load(n) for n in range(chunks)]
    fac_loads[0].start()
    first_loads = [
        load(src, dst, n)
        for n, (src, dst) in enumerate(
            (
                (basis_hbm, basis_in),
                (sel_hbm, sel_ref),
                (q_hbm, q_ref),
                (own_hbm, own_ref),
                (fine_hbm, fine_ref),
                (coarse_hbm.at[seq_pos], coarse),
            )
        )
    ]
    for n in range(1, chunks):
        fac_loads[n].start()
    rk_load = load(rk_hbm, recent_keys, 6)
    rv_load = load(rv_hbm, recent_values, 7)
    sum_load = pltpu.make_async_copy(sum_hbm, summary, i_sem.at[8])
    loads = []
    for g in range(parts):
        at = pl.ds(g * span, span)
        loads.append(pltpu.make_async_copy(pool_hbm.at[at, :], values.at[at, :], v_sem.at[g]))

    barrier = pltpu.get_barrier_semaphore()
    for k in range(seq_count):
        peer = lax.rem(seq_pos + k, seq_count)
        for pool in (core, 1 - core)[k == 0 :]:
            pl.semaphore_signal(
                barrier,
                inc=1,
                device_id={"seq": peer, "pool": pool},
                device_id_type=MESH,
            )

    for copy in first_loads:
        copy.wait()
    fac_loads[0].wait()
    low_half = iota((1, LANES), 1) < HALF
    q_flat = q_ref[...].astype(F32)
    q_rows = jnp.concatenate([q_flat[:, r * HD : (r + 1) * HD] for r in range(rows)], axis=0)
    q_swap = half_swap(q_rows)
    q_pairs = []
    q_plain = []
    for p in range(pairs):
        first = slice(2 * p * gqa, (2 * p + 1) * gqa)
        second = slice((2 * p + 1) * gqa, (2 * p + 2) * gqa)
        x = jnp.concatenate(
            [jnp.where(low_half, q_rows[first], 0.0), jnp.where(low_half, 0.0, q_swap[second])], axis=0
        )
        y = jnp.concatenate(
            [jnp.where(low_half, q_swap[first], 0.0), jnp.where(low_half, 0.0, q_rows[second])], axis=0
        )
        q_pairs.append(jnp.concatenate([x, y], axis=1).astype(BF))
        zero = jnp.zeros((gqa, HD), F32)
        plain = [
            jnp.concatenate([q_rows[first], zero], axis=1),
            jnp.concatenate([zero, q_rows[second]], axis=1),
        ]
        q_plain.append(jnp.concatenate(plain, axis=0).astype(BF))

    sel = jnp.where(core == 0, sel_ref[:heads, :], sel_ref[heads:, :]) - seq_pos * pages
    count = sel.shape[1]
    page_tok = iota((1, pages), 1) * PAGE
    spread_tok = (iota((groups, LANES), 0) * SIXTEEN + iota((groups, LANES), 1) % SIXTEEN) * PAGE
    chosen_rows = []
    for h in range(heads):
        ids = sel[h : h + 1, :]
        hi = jnp.floor_divide(ids, SIXTEEN)
        lo = ids - hi * SIXTEEN
        hit = nt(
            ones_where(iota((groups, count), 0) == hi),
            ones_where(iota((LANES, count), 0) % SIXTEEN == lo),
        )
        live[h] = jnp.where(hit > 0.5, limit - spread_tok, 0)
        by_page = jnp.concatenate([hit[g : g + 1, :SIXTEEN] for g in range(groups)], axis=1)
        chosen_rows.append(jnp.broadcast_to(by_page > 0.5, (gqa, pages)))

    chosen = [jnp.concatenate(chosen_rows[2 * p : 2 * p + 2], axis=0) for p in range(pairs)]
    owners = own_ref[...]
    before = nn(
        ones_where(owners == 1), ones_where(iota((LANES, LANES), 0) < iota((LANES, LANES), 1))
    )
    chunk_total = jnp.sum(owners.astype(F32), axis=1, keepdims=True)
    running = jnp.zeros((1, 1), F32)
    slots = []
    for c in range(chunks):
        ones = before[c : c + 1, :] + running
        running = running + chunk_total[c : c + 1, :]
        page = (iota((1, LANES), 1) + c * LANES).astype(F32)
        slots.append(jnp.where(owners[c : c + 1, :] == 1, ones + pages // 2, page - ones))
    slot = jnp.concatenate(slots, axis=1).astype(jnp.int32)
    slot = slot - (1 - core) * (pages // 2)
    slot = jnp.where(slot < 0, slot + pages, slot)
    place = slot % LANES
    column = slot - place + place % 16 * PAGE + place // 16
    column_t = jnp.swapaxes(
        jnp.concatenate([column[:, c * LANES : (c + 1) * LANES] for c in range(chunks)], axis=0).astype(
            F32
        ),
        0,
        1,
    ).astype(jnp.int32)

    for p in range(pairs):
        a = basis_in[:, 2 * p * HD : (2 * p + 1) * HD].astype(F32)
        b = basis_in[:, (2 * p + 1) * HD : (2 * p + 2) * HD].astype(F32)
        basis[:, 2 * p * HD : (2 * p + 1) * HD] = jnp.where(low_half, a, half_swap(b)).astype(BF)
        basis[:, (2 * p + 1) * HD : (2 * p + 2) * HD] = jnp.where(low_half, half_swap(a), b).astype(BF)

    lane = iota((1, LANES), 1)
    source = iota((rank_dim, LANES), 1)
    slot_of = source // SIXTEEN
    source = source % SIXTEEN * PAGE + jnp.where(
        slot_of % 2 == 0, PAGE // 2 - 1 - slot_of // 2, PAGE // 2 + slot_of // 2
    )
    page_row = iota((SIXTEEN, LANES), 0)
    lane_slot = lane // SIXTEEN
    lane_token = jnp.where(
        lane_slot % 2 == 0, PAGE // 2 - 1 - lane_slot // 2, PAGE // 2 + lane_slot // 2
    )

    def ordered(at, n):
        block = [
            jnp.take_along_axis(fac[:, at + k * LANES : at + (k + 1) * LANES].astype(F32), source, axis=1)
            for k in range(n)
        ]
        return tn(jnp.concatenate(block, axis=1).astype(BF), basis[...])

    def rotated(u, cj, sj, at):
        cm = fine_ref[at : at + SIXTEEN, :]
        sm = fine_ref[GROUP + at : GROUP + at + SIXTEEN, :]
        ca = cj * cm - sj * sm
        sa = sj * cm + cj * sm
        tiles = []
        for k in range(PAGE // 2):
            row = 2 * GROUP + k
            cb = fine_ref[row : row + 1, :]
            sb = fine_ref[row + PAGE // 2 : row + PAGE // 2 + 1, :]
            cc, ss, sc, cs = ca * cb, sa * sb, sa * cb, ca * sb
            for e, cosine, sine in ((0, cc + ss, sc - cs), (1, cc - ss, sc + cs)):
                rows_of = slice((2 * k + e) * SIXTEEN, (2 * k + e + 1) * SIXTEEN)
                cols = []
                for p in range(pairs):
                    x = u[rows_of, 2 * p * HD : (2 * p + 1) * HD]
                    y = u[rows_of, (2 * p + 1) * HD : (2 * p + 2) * HD]
                    cols.append((x * cosine - y * sine).astype(BF))
                    cols.append((y * cosine + x * sine).astype(BF))
                tiles.append(cols)
        return tiles

    def swap_bits(tiles, bits):
        tiles = list(tiles)
        for step, bit in enumerate(bits):
            clear = lane // bit % 2 == 0
            for i in range(PAGE):
                other = i | 1 << step
                if other != i:
                    a, c = tiles[i], tiles[other]
                    tiles[i] = jnp.where(clear, a, pltpu.roll(c, bit, axis=1))
                    tiles[other] = jnp.where(clear, pltpu.roll(a, LANES - bit, axis=1), c)
        return tiles

    def chunk(n, tops, u_next):
        tops = list(tops)
        by_group = [[] for _ in range(pairs)]
        for b in range(span // FINE):
            u = u_next
            j = n * (span // FINE) + b
            u_next = ordered((j + 1) * FINE, FINE // LANES) if (j + 1) * FINE < tokens else None
            cj, sj = coarse[0, j : j + 1, :], coarse[1, j : j + 1, :]
            blocks = [[] for _ in range(pairs)]
            for e in range(FINE // LANES):
                tiles = rotated(u[e * LANES : (e + 1) * LANES, :], cj, sj, e * SIXTEEN)
                g = (n * (span // FINE) + b) * (FINE // LANES) + e
                used = jnp.clip(limit - (g * SIXTEEN + page_row) * PAGE, 0, PAGE).astype(F32).astype(BF)
                for c in range(heads):
                    always = tiles[ORDER.index(0)][c]
                    column_tiles = [
                        t[c] if i == 0 else jnp.where(used > i, t[c], always)
                        for t, i in zip(tiles, ORDER)
                    ]
                    low = functools.reduce(jnp.minimum, column_tiles)
                    high = functools.reduce(jnp.maximum, column_tiles)
                    centers[g * SIXTEEN : (g + 1) * SIXTEEN, c * HD : (c + 1) * HD] = low + high
                for p in range(pairs):
                    blocks[p] += [
                        jnp.concatenate([t[2 * p], t[2 * p + 1]], axis=1) for t in tiles
                    ]
            for p in range(pairs):
                s = nt(q_pairs[p], jnp.concatenate(blocks[p], axis=0)) * scale
                for e in range(FINE // LANES):
                    g = (n * (span // FINE) + b) * (FINE // LANES) + e
                    left = jnp.concatenate(
                        [
                            jnp.broadcast_to(live[h, g : g + 1, :], (gqa, LANES))
                            for h in (2 * p, 2 * p + 1)
                        ],
                        axis=0,
                    )
                    one = jnp.where(
                        left > lane_token, s[:, e * LANES : (e + 1) * LANES], -jnp.inf
                    )
                    tops[p] = jnp.maximum(tops[p], one)
                    by_group[p].append(one)
        for p in range(pairs):
            mine = slice(p * 2 * gqa, (p + 1) * 2 * gqa)
            by_token = swap_bits(by_group[p], (16, 32, 64))
            for i in range(PAGE):
                scores[n, mine, i * LANES : (i + 1) * LANES] = by_token[i]
        wanted = jnp.broadcast_to(column_t[:, n : n + 1], (LANES, LANES))
        for t in range(chunks):
            onehot[n * LANES : (n + 1) * LANES, t * LANES : (t + 1) * LANES] = ones_where(
                wanted == lane + t * LANES
            )
        return tops, u_next

    tops = [jnp.full((2 * gqa, LANES), -1e30, F32)] * pairs
    u_next = ordered(0, FINE // LANES)
    for n in range(chunks):
        if n + 1 < chunks:
            fac_loads[n + 1].wait()
        if n == 0:
            for copy in [sum_load] + loads:
                copy.start()
        tops, u_next = chunk(n, tops, u_next)

    rk_load.wait()
    peaks = []
    recents = []
    for p in range(pairs):
        mine = slice(p * 2 * gqa, (p + 1) * 2 * gqa)
        cols = slice(p * 2 * HD, (p + 1) * 2 * HD)
        s = nt(q_pairs[p], centers[:, cols]) * (scale * 0.5)
        s = jnp.where((page_tok < limit) & jnp.logical_not(chosen[p]), s, -jnp.inf)
        land[mine, :] = s
        recent = nt(q_plain[p], recent_keys[:, cols]) * scale
        first = jnp.zeros(recent.shape, jnp.int32) + seq_pos
        recent = jnp.where(first == 0, recent, -jnp.inf)
        recents.append(recent)
        best = jnp.maximum(jnp.max(tops[p], axis=1, keepdims=True), jnp.max(s, axis=1, keepdims=True))
        peaks.append(jnp.maximum(best, jnp.max(recent, axis=1, keepdims=True)))

    totals = [jnp.zeros((2 * gqa, LANES), F32)] * pairs
    for n in range(chunks):
        for p in range(pairs):
            mine = slice(p * 2 * gqa, (p + 1) * 2 * gqa)
            for i in range(PAGE):
                w = jnp.exp2(scores[n, mine, i * LANES : (i + 1) * LANES] - peaks[p])
                totals[p] = totals[p] + w
                row = i * rows + p * 2 * gqa
                wbuf[row : row + 2 * gqa, n * LANES : (n + 1) * LANES] = w.astype(BF)

    def regroup(moved, ref):
        for t in range(pages // 2 // LANES):
            for b in range(rows // 16):
                by_token = [None] * PAGE
                for place_of, i in enumerate(ORDER):
                    row = place_of * rows + b * SIXTEEN
                    by_token[i] = moved[row : row + SIXTEEN, t * LANES : (t + 1) * LANES].astype(BF)
                by_lane = swap_bits(by_token, (1, 2, 4))
                for i in range(PAGE):
                    at = t * span + i * LANES
                    ref[b * SIXTEEN : (b + 1) * SIXTEEN, at : at + LANES] = by_lane[i]

    regroup(nn(wbuf[...], onehot[:, 0 : pages // 2]), outgoing)

    def copy_to(src, dst, sems, device):
        copy = pltpu.make_async_remote_copy(
            src_ref=src,
            dst_ref=dst,
            send_sem=sems[0],
            recv_sem=sems[1],
            device_id=device,
            device_id_type=MESH,
        )
        copy.start()
        return copy

    def spread(src, dst, n, pool, begin):
        return [
            copy_to(
                src,
                dst,
                (send_sem.at[n, k], recv_sem.at[n, k]),
                {"seq": lax.rem(seq_pos + k, seq_count), "pool": pool},
            )
            for k in range(begin, seq_count)
        ]

    pl.semaphore_wait(barrier, 2 * seq_count - 1)
    swap = copy_to(outgoing, theirs, (pair_sem.at[0], pair_sem.at[1]), partner)
    regroup(nn(wbuf[...], onehot[:, pages // 2 : pages]), own_w)

    at_lane = iota((rows, LANES), 0) == iota((rows, LANES), 1)
    land_w = []
    recent_w = []
    sums = []
    for p in range(pairs):
        mine = slice(p * 2 * gqa, (p + 1) * 2 * gqa)
        w = jnp.exp2(land[mine, :] - peaks[p])
        r = jnp.exp2(recents[p] - peaks[p])
        sums.append(
            jnp.sum(w, axis=1, keepdims=True)
            + jnp.sum(totals[p], axis=1, keepdims=True)
            + jnp.sum(r, axis=1, keepdims=True)
        )
        land_w.append(w.astype(BF))
        recent_w.append(r.astype(BF))
    as_rows = [
        jnp.sum(
            jnp.where(at_lane, jnp.concatenate(col_of, axis=0), 0.0), axis=0, keepdims=True
        )
        for col_of in (peaks, sums)
    ]
    stats[seq_pos] = jnp.concatenate(as_rows + [jnp.zeros((6, LANES), F32)], axis=0)
    stat_sends = spread(stats.at[seq_pos], stats.at[seq_pos], 0, core, 1)

    def diagonal(blocks):
        return jnp.concatenate(
            [
                blocks[h // 2][h % 2 * gqa : (h % 2 + 1) * gqa, h % 2 * HD : (h % 2 + 1) * HD]
                for h in range(heads)
            ],
            axis=0,
        )

    def weighted(ref, p, g, first):
        cols = pl.ds(pl.multiple_of(first + p * 2 * HD, 2 * HD), 2 * HD)
        return nn(
            ref[p * 2 * gqa : (p + 1) * 2 * gqa, g * span : (g + 1) * span],
            values[g * span : (g + 1) * span, cols],
        )

    rv_load.wait()
    sum_load.wait()
    mine = []
    for p in range(pairs):
        cols = slice(p * 2 * HD, (p + 1) * 2 * HD)
        mine.append(nn(land_w[p], summary[:, cols]) + nn(recent_w[p], recent_values[:, cols]))
    for g in range(parts):
        loads[g].wait()
        for p in range(pairs):
            mine[p] = mine[p] + weighted(own_w, p, g, core * width)
    bodies[core, seq_pos] = diagonal(mine).astype(BF)
    sends = spread(bodies.at[core, seq_pos], bodies.at[core, seq_pos], 1, core, 1)
    swap.wait()
    other = [jnp.zeros((2 * gqa, 2 * HD), F32)] * pairs
    for g in range(parts):
        for p in range(pairs):
            other[p] = other[p] + weighted(theirs, p, g, (1 - core) * width)
    other_out[...] = diagonal(other).astype(BF)
    sends = sends + spread(other_out, bodies.at[core, seq_pos], 2, 1 - core, 0)

    for send in stat_sends:
        send.wait()
    peak_rows = [stats[k, 0:1, :] for k in range(seq_count)]
    joint = functools.reduce(jnp.maximum, peak_rows)

    def column_of(row):
        return jnp.sum(jnp.where(at_lane, row, 0.0), axis=1, keepdims=True)

    weight_sum = jnp.zeros((1, LANES), F32)
    factors = []
    for k in range(seq_count):
        factor = jnp.exp2(peak_rows[k] - joint)
        weight_sum = weight_sum + stats[k, 1:2, :] * factor
        factors.append(factor)
    inverse = 1.0 / weight_sum
    factors = [column_of(factor * inverse) for factor in factors]
    for send in sends:
        send.wait()
    result = jnp.zeros((rows, LANES), F32)
    for k in range(seq_count):
        result = result + (bodies[0, k].astype(F32) + bodies[1, k].astype(F32)) * factors[k]
    out_ref[...] = jnp.concatenate([result[r : r + 1, :] for r in range(rows)], axis=1).astype(BF)


def local(
    seq_count,
    factors,
    basis,
    value_pool,
    page_summary,
    recent_keys,
    recent_values,
    query,
    selected,
    owner_map,
    lengths,
):
    tokens, rank_dim = factors.shape[1:]
    width = basis.shape[2]
    heads = width // HD
    rows = query.shape[1] // HD
    pages = tokens // PAGE
    chunks = pages // LANES
    span = LANES * PAGE
    parts = value_pool.shape[1] // span
    coarse, fine = [jnp.asarray(t) for t in angle_tables(tokens * seq_count, seq_count)]
    vmem = pl.BlockSpec(memory_space=pltpu.VMEM)
    hbm = pl.BlockSpec(memory_space=pl.ANY)
    dma = pltpu.SemaphoreType.DMA
    return pl.pallas_call(
        functools.partial(attention_kernel, heads, seq_count),
        out_shape=jax.ShapeDtypeStruct((1, rows * HD), BF),
        in_specs=[pl.BlockSpec(memory_space=pltpu.SMEM)] + [hbm] * 11,
        out_specs=vmem,
        scratch_shapes=[
            pltpu.VMEM(query.shape, BF),
            pltpu.VMEM(selected.shape[1:], jnp.int32),
            pltpu.VMEM((chunks, LANES), jnp.int32),
            pltpu.VMEM(fine.shape, F32),
            pltpu.VMEM(coarse.shape[1:], F32),
            pltpu.VMEM((rank_dim, width), BF),
            pltpu.VMEM((WIN, width), BF),
            pltpu.VMEM((WIN, width), BF),
            pltpu.VMEM((rank_dim, tokens), BF),
            pltpu.VMEM((pages, width), BF),
            pltpu.VMEM(value_pool.shape[1:], BF),
            pltpu.VMEM((rank_dim, width), BF),
            pltpu.VMEM((pages, width), BF),
            pltpu.VMEM((heads, tokens // LANES, LANES), jnp.int32),
            pltpu.VMEM((chunks, rows, span), F32),
            pltpu.VMEM((rows, pages), F32),
            pltpu.VMEM((PAGE * rows, pages), BF),
            pltpu.VMEM((pages, pages), BF),
            pltpu.VMEM((rows, parts * span), BF),
            pltpu.VMEM((rows, parts * span), BF),
            pltpu.VMEM((rows, parts * span), BF),
            pltpu.VMEM((rows, LANES), BF),
            pltpu.VMEM((2, seq_count, rows, LANES), BF),
            pltpu.VMEM((seq_count, 8, LANES), F32),
            dma((chunks,)),
            dma((9,)),
            dma((parts,)),
            dma((2,)),
            dma((3, seq_count)),
            dma((3, seq_count)),
        ],
        compiler_params=pltpu.CompilerParams(
            collective_id=0, has_side_effects=True, vmem_limit_bytes=60 * 1024 * 1024
        ),
    )(
        lengths,
        query,
        selected[0],
        owner_map.reshape(chunks, LANES),
        fine,
        coarse,
        basis[0],
        recent_keys[0],
        recent_values[0],
        jnp.swapaxes(factors[0], 0, 1),
        page_summary[0],
        value_pool[0],
    )


def solution(mesh):
    placed = (
        P("grp", "seq", None),
        P("grp", None, "pool"),
        P("grp", ("seq", "pool"), None),
        P("grp", "seq", "pool"),
        P("grp", None, "pool"),
        P("grp", None, "pool"),
        P("grp", "pool"),
        P("grp", None, None),
        P("grp", "seq"),
        P("grp"),
    )
    return jax.shard_map(
        functools.partial(local, mesh.shape["seq"]),
        mesh=mesh,
        in_specs=placed,
        out_specs=P("grp", "pool"),
        check_vma=False,
    )
```

```python
import functools
import math

import jax
import jax.numpy as jnp
import numpy as np
from jax import lax
from jax.experimental import pallas as pl
from jax.experimental.pallas import tpu as pltpu
from jax.sharding import PartitionSpec as P

HD = 128
PAGE = 8
WIN = 64
LANES = 128
FINE = 256
HALF = HD // 2
SIXTEEN = 16
ORDER = (3, 4, 2, 5, 1, 6, 0, 7)
GROUP = FINE // PAGE
MESH = pl.DeviceIdType.MESH
BF = jnp.bfloat16
F32 = jnp.float32


def llama_rates(head_dim):
    half_dim = head_dim // 2
    base_rates = 500000.0 ** (-(np.arange(half_dim) * 2.0) / head_dim)
    wavelen = 2.0 * math.pi / base_rates
    smooth = (8192.0 / wavelen - 1.0) / 3.0
    blended = (1.0 - smooth) * base_rates / 8.0 + smooth * base_rates
    return np.where(
        wavelen < 2048.0, base_rates, np.where(wavelen > 8192.0, base_rates / 8.0, blended)
    )


def angle_tables(length, seq_count):
    rates = llama_rates(HD)

    def pair(angles):
        return [np.concatenate([f(angles)] * 2, axis=1) for f in (np.cos, np.sin)]

    coarse = pair((np.arange(length // FINE) * float(FINE))[:, None] * rates[None, :])
    coarse = np.stack([t.reshape(seq_count, -1, HD) for t in coarse], axis=1)
    middle = pair((np.arange(GROUP) * float(PAGE) + (PAGE - 1) * 0.5)[:, None] * rates[None, :])
    inner = pair((np.arange(PAGE // 2) + 0.5)[:, None] * rates[None, :])
    return coarse.astype(np.float32), np.concatenate(middle + inner, axis=0).astype(np.float32)


def nt(a, b):
    return lax.dot_general(a, b, (((1,), (1,)), ((), ())), preferred_element_type=F32)


def tn(a, b):
    return lax.dot_general(a, b, (((0,), (0,)), ((), ())), preferred_element_type=F32)


def nn(a, b):
    return jnp.dot(a, b, preferred_element_type=F32)


def ones_where(mask):
    return jnp.where(mask, 1.0, 0.0).astype(BF)


def iota(shape, dim):
    return lax.broadcasted_iota(jnp.int32, shape, dim)


def half_swap(x):
    return pltpu.roll(x, HALF, axis=1)


def attention_kernel(
    heads,
    seq_count,
    len_ref,
    q_hbm,
    sel_hbm,
    own_hbm,
    fine_hbm,
    coarse_hbm,
    basis_hbm,
    rk_hbm,
    rv_hbm,
    fac_hbm,
    sum_hbm,
    pool_hbm,
    out_ref,
    q_ref,
    sel_ref,
    own_ref,
    fine_ref,
    coarse,
    basis_in,
    recent_keys,
    recent_values,
    fac,
    summary,
    values,
    basis,
    centers,
    live,
    scores,
    land,
    wbuf,
    onehot,
    outgoing,
    own_w,
    theirs,
    other_out,
    bodies,
    stats,
    f_sem,
    i_sem,
    v_sem,
    pair_sem,
    send_sem,
    recv_sem,
):
    seq_pos = lax.axis_index("seq")
    core = lax.axis_index("pool")
    rows = q_ref.shape[1] // HD
    gqa = rows // heads
    pairs = heads // 2
    width = heads * HD
    tokens = fac.shape[1]
    pages = tokens // PAGE
    chunks = pages // LANES
    span = LANES * PAGE
    groups = tokens // LANES
    rank_dim = fac.shape[0]
    parts = values.shape[0] // span
    limit = len_ref[0] - seq_pos * tokens
    scale = HD ** (-0.5) * math.log2(math.e)
    partner = {"pool": 1 - core}

    def fac_load(n):
        at = pl.ds(n * span, span)
        return pltpu.make_async_copy(fac_hbm.at[:, at], fac.at[:, at], f_sem.at[n])

    def load(src, dst, n):
        copy = pltpu.make_async_copy(src, dst, i_sem.at[n])
        copy.start()
        return copy

    fac_loads = [fac_load(n) for n in range(chunks)]
    fac_loads[0].start()
    first_loads = [
        load(src, dst, n)
        for n, (src, dst) in enumerate(
            (
                (basis_hbm, basis_in),
                (sel_hbm, sel_ref),
                (q_hbm, q_ref),
                (own_hbm, own_ref),
                (fine_hbm, fine_ref),
                (coarse_hbm.at[seq_pos], coarse),
            )
        )
    ]
    for n in range(1, chunks):
        fac_loads[n].start()
    rk_load = load(rk_hbm, recent_keys, 6)
    rv_load = load(rv_hbm, recent_values, 7)
    sum_load = pltpu.make_async_copy(sum_hbm, summary, i_sem.at[8])
    loads = []
    for g in range(parts):
        at = pl.ds(g * span, span)
        loads.append(pltpu.make_async_copy(pool_hbm.at[at, :], values.at[at, :], v_sem.at[g]))

    barrier = pltpu.get_barrier_semaphore()
    for k in range(seq_count):
        peer = lax.rem(seq_pos + k, seq_count)
        for pool in (core, 1 - core)[k == 0 :]:
            pl.semaphore_signal(
                barrier,
                inc=1,
                device_id={"seq": peer, "pool": pool},
                device_id_type=MESH,
            )

    for copy in first_loads:
        copy.wait()
    low_half = iota((1, LANES), 1) < HALF
    q_flat = q_ref[...].astype(F32)
    q_rows = jnp.concatenate([q_flat[:, r * HD : (r + 1) * HD] for r in range(rows)], axis=0)
    q_swap = half_swap(q_rows)
    q_pairs = []
    q_plain = []
    for p in range(pairs):
        first = slice(2 * p * gqa, (2 * p + 1) * gqa)
        second = slice((2 * p + 1) * gqa, (2 * p + 2) * gqa)
        x = jnp.concatenate(
            [jnp.where(low_half, q_rows[first], 0.0), jnp.where(low_half, 0.0, q_swap[second])], axis=0
        )
        y = jnp.concatenate(
            [jnp.where(low_half, q_swap[first], 0.0), jnp.where(low_half, 0.0, q_rows[second])], axis=0
        )
        q_pairs.append(jnp.concatenate([x, y], axis=1).astype(BF))
        zero = jnp.zeros((gqa, HD), F32)
        plain = [
            jnp.concatenate([q_rows[first], zero], axis=1),
            jnp.concatenate([zero, q_rows[second]], axis=1),
        ]
        q_plain.append(jnp.concatenate(plain, axis=0).astype(BF))

    sel = jnp.where(core == 0, sel_ref[:heads, :], sel_ref[heads:, :]) - seq_pos * pages
    count = sel.shape[1]
    page_tok = iota((1, pages), 1) * PAGE
    spread_tok = (iota((groups, LANES), 0) * SIXTEEN + iota((groups, LANES), 1) % SIXTEEN) * PAGE
    chosen_rows = []
    for h in range(heads):
        ids = sel[h : h + 1, :]
        hi = jnp.floor_divide(ids, SIXTEEN)
        lo = ids - hi * SIXTEEN
        hit = nt(
            ones_where(iota((groups, count), 0) == hi),
            ones_where(iota((LANES, count), 0) % SIXTEEN == lo),
        )
        live[h] = jnp.where(hit > 0.5, limit - spread_tok, 0)
        by_page = jnp.concatenate([hit[g : g + 1, :SIXTEEN] for g in range(groups)], axis=1)
        chosen_rows.append(jnp.broadcast_to(by_page > 0.5, (gqa, pages)))

    chosen = [jnp.concatenate(chosen_rows[2 * p : 2 * p + 2], axis=0) for p in range(pairs)]
    owners = own_ref[...]
    before = nn(
        ones_where(owners == 1), ones_where(iota((LANES, LANES), 0) < iota((LANES, LANES), 1))
    )
    chunk_total = jnp.sum(owners.astype(F32), axis=1, keepdims=True)
    running = jnp.zeros((1, 1), F32)
    slots = []
    for c in range(chunks):
        ones = before[c : c + 1, :] + running
        running = running + chunk_total[c : c + 1, :]
        page = (iota((1, LANES), 1) + c * LANES).astype(F32)
        slots.append(jnp.where(owners[c : c + 1, :] == 1, ones + pages // 2, page - ones))
    slot = jnp.concatenate(slots, axis=1).astype(jnp.int32)
    slot = slot - (1 - core) * (pages // 2)
    slot = jnp.where(slot < 0, slot + pages, slot)
    place = slot % LANES
    column = slot - place + place % 16 * PAGE + place // 16
    column_t = jnp.swapaxes(
        jnp.concatenate([column[:, c * LANES : (c + 1) * LANES] for c in range(chunks)], axis=0).astype(
            F32
        ),
        0,
        1,
    ).astype(jnp.int32)

    for p in range(pairs):
        a = basis_in[:, 2 * p * HD : (2 * p + 1) * HD].astype(F32)
        b = basis_in[:, (2 * p + 1) * HD : (2 * p + 2) * HD].astype(F32)
        basis[:, 2 * p * HD : (2 * p + 1) * HD] = jnp.where(low_half, a, half_swap(b)).astype(BF)
        basis[:, (2 * p + 1) * HD : (2 * p + 2) * HD] = jnp.where(low_half, half_swap(a), b).astype(BF)

    lane = iota((1, LANES), 1)
    source = iota((rank_dim, LANES), 1)
    slot_of = source // SIXTEEN
    source = source % SIXTEEN * PAGE + jnp.where(
        slot_of % 2 == 0, PAGE // 2 - 1 - slot_of // 2, PAGE // 2 + slot_of // 2
    )
    page_row = iota((SIXTEEN, LANES), 0)
    lane_slot = lane // SIXTEEN
    lane_token = jnp.where(
        lane_slot % 2 == 0, PAGE // 2 - 1 - lane_slot // 2, PAGE // 2 + lane_slot // 2
    )

    def ordered(at, n):
        block = [
            jnp.take_along_axis(fac[:, at + k * LANES : at + (k + 1) * LANES].astype(F32), source, axis=1)
            for k in range(n)
        ]
        return tn(jnp.concatenate(block, axis=1).astype(BF), basis[...])

    def rotated(u, cj, sj, at):
        cm = fine_ref[at : at + SIXTEEN, :]
        sm = fine_ref[GROUP + at : GROUP + at + SIXTEEN, :]
        ca = cj * cm - sj * sm
        sa = sj * cm + cj * sm
        tiles = []
        for k in range(PAGE // 2):
            row = 2 * GROUP + k
            cb = fine_ref[row : row + 1, :]
            sb = fine_ref[row + PAGE // 2 : row + PAGE // 2 + 1, :]
            cc, ss, sc, cs = ca * cb, sa * sb, sa * cb, ca * sb
            for e, cosine, sine in ((0, cc + ss, sc - cs), (1, cc - ss, sc + cs)):
                rows_of = slice((2 * k + e) * SIXTEEN, (2 * k + e + 1) * SIXTEEN)
                cols = []
                for p in range(pairs):
                    x = u[rows_of, 2 * p * HD : (2 * p + 1) * HD]
                    y = u[rows_of, (2 * p + 1) * HD : (2 * p + 2) * HD]
                    cols.append((x * cosine - y * sine).astype(BF))
                    cols.append((y * cosine + x * sine).astype(BF))
                tiles.append(cols)
        return tiles

    def swap_bits(tiles, bits):
        tiles = list(tiles)
        for step, bit in enumerate(bits):
            clear = lane // bit % 2 == 0
            for i in range(PAGE):
                other = i | 1 << step
                if other != i:
                    a, c = tiles[i], tiles[other]
                    tiles[i] = jnp.where(clear, a, pltpu.roll(c, bit, axis=1))
                    tiles[other] = jnp.where(clear, pltpu.roll(a, LANES - bit, axis=1), c)
        return tiles

    def chunk(n, tops, u_next):
        tops = list(tops)
        by_group = [[] for _ in range(pairs)]
        for b in range(span // FINE):
            u = u_next
            j = n * (span // FINE) + b
            u_next = ordered((j + 1) * FINE, FINE // LANES) if (j + 1) * FINE < tokens else None
            cj, sj = coarse[0, j : j + 1, :], coarse[1, j : j + 1, :]
            blocks = [[] for _ in range(pairs)]
            for e in range(FINE // LANES):
                tiles = rotated(u[e * LANES : (e + 1) * LANES, :], cj, sj, e * SIXTEEN)
                g = (n * (span // FINE) + b) * (FINE // LANES) + e
                used = jnp.clip(limit - (g * SIXTEEN + page_row) * PAGE, 0, PAGE).astype(F32).astype(BF)
                for c in range(heads):
                    always = tiles[ORDER.index(0)][c]
                    column_tiles = [
                        t[c] if i == 0 else jnp.where(used > i, t[c], always)
                        for t, i in zip(tiles, ORDER)
                    ]
                    low = functools.reduce(jnp.minimum, column_tiles)
                    high = functools.reduce(jnp.maximum, column_tiles)
                    centers[g * SIXTEEN : (g + 1) * SIXTEEN, c * HD : (c + 1) * HD] = low + high
                for p in range(pairs):
                    blocks[p] += [
                        jnp.concatenate([t[2 * p], t[2 * p + 1]], axis=1) for t in tiles
                    ]
            for p in range(pairs):
                s = nt(q_pairs[p], jnp.concatenate(blocks[p], axis=0)) * scale
                for e in range(FINE // LANES):
                    g = (n * (span // FINE) + b) * (FINE // LANES) + e
                    left = jnp.concatenate(
                        [
                            jnp.broadcast_to(live[h, g : g + 1, :], (gqa, LANES))
                            for h in (2 * p, 2 * p + 1)
                        ],
                        axis=0,
                    )
                    one = jnp.where(
                        left > lane_token, s[:, e * LANES : (e + 1) * LANES], -jnp.inf
                    )
                    tops[p] = jnp.maximum(tops[p], one)
                    by_group[p].append(one)
        for p in range(pairs):
            mine = slice(p * 2 * gqa, (p + 1) * 2 * gqa)
            by_token = swap_bits(by_group[p], (16, 32, 64))
            for i in range(PAGE):
                scores[n, mine, i * LANES : (i + 1) * LANES] = by_token[i]
        wanted = jnp.broadcast_to(column_t[:, n : n + 1], (LANES, LANES))
        for t in range(chunks):
            onehot[n * LANES : (n + 1) * LANES, t * LANES : (t + 1) * LANES] = ones_where(
                wanted == lane + t * LANES
            )
        return tops, u_next

    tops = [jnp.full((2 * gqa, LANES), -1e30, F32)] * pairs
    for copy in fac_loads[:-1]:
        copy.wait()
    for copy in [sum_load] + loads:
        copy.start()
    fac_loads[-1].wait()
    u_next = ordered(0, FINE // LANES)
    for n in range(chunks):
        tops, u_next = chunk(n, tops, u_next)

    rk_load.wait()
    peaks = []
    recents = []
    for p in range(pairs):
        mine = slice(p * 2 * gqa, (p + 1) * 2 * gqa)
        cols = slice(p * 2 * HD, (p + 1) * 2 * HD)
        s = nt(q_pairs[p], centers[:, cols]) * (scale * 0.5)
        s = jnp.where((page_tok < limit) & jnp.logical_not(chosen[p]), s, -jnp.inf)
        land[mine, :] = s
        recent = nt(q_plain[p], recent_keys[:, cols]) * scale
        first = jnp.zeros(recent.shape, jnp.int32) + seq_pos
        recent = jnp.where(first == 0, recent, -jnp.inf)
        recents.append(recent)
        best = jnp.maximum(jnp.max(tops[p], axis=1, keepdims=True), jnp.max(s, axis=1, keepdims=True))
        peaks.append(jnp.maximum(best, jnp.max(recent, axis=1, keepdims=True)))

    totals = [jnp.zeros((2 * gqa, LANES), F32)] * pairs
    for n in range(chunks):
        for p in range(pairs):
            mine = slice(p * 2 * gqa, (p + 1) * 2 * gqa)
            for i in range(PAGE):
                w = jnp.exp2(scores[n, mine, i * LANES : (i + 1) * LANES] - peaks[p])
                totals[p] = totals[p] + w
                row = i * rows + p * 2 * gqa
                wbuf[row : row + 2 * gqa, n * LANES : (n + 1) * LANES] = w.astype(BF)

    def regroup(moved, ref):
        for t in range(pages // 2 // LANES):
            for b in range(rows // 16):
                by_token = [None] * PAGE
                for place_of, i in enumerate(ORDER):
                    row = place_of * rows + b * SIXTEEN
                    by_token[i] = moved[row : row + SIXTEEN, t * LANES : (t + 1) * LANES].astype(BF)
                by_lane = swap_bits(by_token, (1, 2, 4))
                for i in range(PAGE):
                    at = t * span + i * LANES
                    ref[b * SIXTEEN : (b + 1) * SIXTEEN, at : at + LANES] = by_lane[i]

    regroup(nn(wbuf[...], onehot[:, 0 : pages // 2]), outgoing)

    def copy_to(src, dst, sems, device):
        copy = pltpu.make_async_remote_copy(
            src_ref=src,
            dst_ref=dst,
            send_sem=sems[0],
            recv_sem=sems[1],
            device_id=device,
            device_id_type=MESH,
        )
        copy.start()
        return copy

    def spread(src, dst, n, pool, begin):
        return [
            copy_to(
                src,
                dst,
                (send_sem.at[n, k], recv_sem.at[n, k]),
                {"seq": lax.rem(seq_pos + k, seq_count), "pool": pool},
            )
            for k in range(begin, seq_count)
        ]

    pl.semaphore_wait(barrier, 2 * seq_count - 1)
    swap = copy_to(outgoing, theirs, (pair_sem.at[0], pair_sem.at[1]), partner)
    regroup(nn(wbuf[...], onehot[:, pages // 2 : pages]), own_w)

    at_lane = iota((rows, LANES), 0) == iota((rows, LANES), 1)
    land_w = []
    recent_w = []
    sums = []
    for p in range(pairs):
        mine = slice(p * 2 * gqa, (p + 1) * 2 * gqa)
        w = jnp.exp2(land[mine, :] - peaks[p])
        r = jnp.exp2(recents[p] - peaks[p])
        sums.append(
            jnp.sum(w, axis=1, keepdims=True)
            + jnp.sum(totals[p], axis=1, keepdims=True)
            + jnp.sum(r, axis=1, keepdims=True)
        )
        land_w.append(w.astype(BF))
        recent_w.append(r.astype(BF))
    as_rows = [
        jnp.sum(
            jnp.where(at_lane, jnp.concatenate(col_of, axis=0), 0.0), axis=0, keepdims=True
        )
        for col_of in (peaks, sums)
    ]
    stats[seq_pos] = jnp.concatenate(as_rows + [jnp.zeros((6, LANES), F32)], axis=0)
    stat_sends = spread(stats.at[seq_pos], stats.at[seq_pos], 0, core, 1)

    def diagonal(blocks):
        return jnp.concatenate(
            [
                blocks[h // 2][h % 2 * gqa : (h % 2 + 1) * gqa, h % 2 * HD : (h % 2 + 1) * HD]
                for h in range(heads)
            ],
            axis=0,
        )

    def weighted(ref, p, g, first):
        cols = pl.ds(pl.multiple_of(first + p * 2 * HD, 2 * HD), 2 * HD)
        return nn(
            ref[p * 2 * gqa : (p + 1) * 2 * gqa, g * span : (g + 1) * span],
            values[g * span : (g + 1) * span, cols],
        )

    rv_load.wait()
    sum_load.wait()
    mine = []
    for p in range(pairs):
        cols = slice(p * 2 * HD, (p + 1) * 2 * HD)
        mine.append(nn(land_w[p], summary[:, cols]) + nn(recent_w[p], recent_values[:, cols]))
    for g in range(parts):
        loads[g].wait()
        for p in range(pairs):
            mine[p] = mine[p] + weighted(own_w, p, g, core * width)
    bodies[core, seq_pos] = diagonal(mine).astype(BF)
    sends = spread(bodies.at[core, seq_pos], bodies.at[core, seq_pos], 1, core, 1)
    swap.wait()
    other = [jnp.zeros((2 * gqa, 2 * HD), F32)] * pairs
    for g in range(parts):
        for p in range(pairs):
            other[p] = other[p] + weighted(theirs, p, g, (1 - core) * width)
    other_out[...] = diagonal(other).astype(BF)
    sends = sends + spread(other_out, bodies.at[core, seq_pos], 2, 1 - core, 0)

    for send in stat_sends:
        send.wait()
    peak_rows = [stats[k, 0:1, :] for k in range(seq_count)]
    joint = functools.reduce(jnp.maximum, peak_rows)

    def column_of(row):
        return jnp.sum(jnp.where(at_lane, row, 0.0), axis=1, keepdims=True)

    weight_sum = jnp.zeros((1, LANES), F32)
    factors = []
    for k in range(seq_count):
        factor = jnp.exp2(peak_rows[k] - joint)
        weight_sum = weight_sum + stats[k, 1:2, :] * factor
        factors.append(factor)
    inverse = 1.0 / weight_sum
    factors = [column_of(factor * inverse) for factor in factors]
    for send in sends:
        send.wait()
    result = jnp.zeros((rows, LANES), F32)
    for k in range(seq_count):
        result = result + (bodies[0, k].astype(F32) + bodies[1, k].astype(F32)) * factors[k]
    out_ref[...] = jnp.concatenate([result[r : r + 1, :] for r in range(rows)], axis=1).astype(BF)


def local(
    seq_count,
    factors,
    basis,
    value_pool,
    page_summary,
    recent_keys,
    recent_values,
    query,
    selected,
    owner_map,
    lengths,
):
    tokens, rank_dim = factors.shape[1:]
    width = basis.shape[2]
    heads = width // HD
    rows = query.shape[1] // HD
    pages = tokens // PAGE
    chunks = pages // LANES
    span = LANES * PAGE
    parts = value_pool.shape[1] // span
    coarse, fine = [jnp.asarray(t) for t in angle_tables(tokens * seq_count, seq_count)]
    vmem = pl.BlockSpec(memory_space=pltpu.VMEM)
    hbm = pl.BlockSpec(memory_space=pl.ANY)
    dma = pltpu.SemaphoreType.DMA
    return pl.pallas_call(
        functools.partial(attention_kernel, heads, seq_count),
        out_shape=jax.ShapeDtypeStruct((1, rows * HD), BF),
        in_specs=[pl.BlockSpec(memory_space=pltpu.SMEM)] + [hbm] * 11,
        out_specs=vmem,
        scratch_shapes=[
            pltpu.VMEM(query.shape, BF),
            pltpu.VMEM(selected.shape[1:], jnp.int32),
            pltpu.VMEM((chunks, LANES), jnp.int32),
            pltpu.VMEM(fine.shape, F32),
            pltpu.VMEM(coarse.shape[1:], F32),
            pltpu.VMEM((rank_dim, width), BF),
            pltpu.VMEM((WIN, width), BF),
            pltpu.VMEM((WIN, width), BF),
            pltpu.VMEM((rank_dim, tokens), BF),
            pltpu.VMEM((pages, width), BF),
            pltpu.VMEM(value_pool.shape[1:], BF),
            pltpu.VMEM((rank_dim, width), BF),
            pltpu.VMEM((pages, width), BF),
            pltpu.VMEM((heads, tokens // LANES, LANES), jnp.int32),
            pltpu.VMEM((chunks, rows, span), F32),
            pltpu.VMEM((rows, pages), F32),
            pltpu.VMEM((PAGE * rows, pages), BF),
            pltpu.VMEM((pages, pages), BF),
            pltpu.VMEM((rows, parts * span), BF),
            pltpu.VMEM((rows, parts * span), BF),
            pltpu.VMEM((rows, parts * span), BF),
            pltpu.VMEM((rows, LANES), BF),
            pltpu.VMEM((2, seq_count, rows, LANES), BF),
            pltpu.VMEM((seq_count, 8, LANES), F32),
            dma((chunks,)),
            dma((9,)),
            dma((parts,)),
            dma((2,)),
            dma((3, seq_count)),
            dma((3, seq_count)),
        ],
        compiler_params=pltpu.CompilerParams(
            collective_id=0, has_side_effects=True, vmem_limit_bytes=60 * 1024 * 1024
        ),
    )(
        lengths,
        query,
        selected[0],
        owner_map.reshape(chunks, LANES),
        fine,
        coarse,
        basis[0],
        recent_keys[0],
        recent_values[0],
        jnp.swapaxes(factors[0], 0, 1),
        page_summary[0],
        value_pool[0],
    )


def solution(mesh):
    placed = (
        P("grp", "seq", None),
        P("grp", None, "pool"),
        P("grp", ("seq", "pool"), None),
        P("grp", "seq", "pool"),
        P("grp", None, "pool"),
        P("grp", None, "pool"),
        P("grp", "pool"),
        P("grp", None, None),
        P("grp", "seq"),
        P("grp"),
    )
    return jax.shard_map(
        functools.partial(local, mesh.shape["seq"]),
        mesh=mesh,
        in_specs=placed,
        out_specs=P("grp", "pool"),
        check_vma=False,
    )
```

```python
import functools
import math

import jax
import jax.numpy as jnp
import numpy as np
from jax import lax
from jax.experimental import pallas as pl
from jax.experimental.pallas import tpu as pltpu
from jax.sharding import PartitionSpec as P

HD = 128
PAGE = 8
WIN = 64
LANES = 128
FINE = 256
HALF = HD // 2
SIXTEEN = 16
ORDER = (3, 4, 2, 5, 1, 6, 0, 7)
GROUP = FINE // PAGE
MESH = pl.DeviceIdType.MESH
BF = jnp.bfloat16
F32 = jnp.float32


def llama_rates(head_dim):
    half_dim = head_dim // 2
    base_rates = 500000.0 ** (-(np.arange(half_dim) * 2.0) / head_dim)
    wavelen = 2.0 * math.pi / base_rates
    smooth = (8192.0 / wavelen - 1.0) / 3.0
    blended = (1.0 - smooth) * base_rates / 8.0 + smooth * base_rates
    return np.where(
        wavelen < 2048.0, base_rates, np.where(wavelen > 8192.0, base_rates / 8.0, blended)
    )


def angle_tables(length, seq_count):
    rates = llama_rates(HD)

    def pair(angles):
        return [np.concatenate([f(angles)] * 2, axis=1) for f in (np.cos, np.sin)]

    coarse = pair((np.arange(length // FINE) * float(FINE))[:, None] * rates[None, :])
    coarse = np.stack([t.reshape(seq_count, -1, HD) for t in coarse], axis=1)
    middle = pair((np.arange(GROUP) * float(PAGE) + (PAGE - 1) * 0.5)[:, None] * rates[None, :])
    inner = pair((np.arange(PAGE // 2) + 0.5)[:, None] * rates[None, :])
    return coarse.astype(np.float32), np.concatenate(middle + inner, axis=0).astype(np.float32)


def nt(a, b):
    return lax.dot_general(a, b, (((1,), (1,)), ((), ())), preferred_element_type=F32)


def tn(a, b):
    return lax.dot_general(a, b, (((0,), (0,)), ((), ())), preferred_element_type=F32)


def nn(a, b):
    return jnp.dot(a, b, preferred_element_type=F32)


def ones_where(mask):
    return jnp.where(mask, 1.0, 0.0).astype(BF)


def iota(shape, dim):
    return lax.broadcasted_iota(jnp.int32, shape, dim)


def half_swap(x):
    return pltpu.roll(x, HALF, axis=1)


def attention_kernel(
    heads,
    seq_count,
    len_ref,
    q_hbm,
    sel_hbm,
    own_hbm,
    fine_hbm,
    coarse_hbm,
    basis_hbm,
    rk_hbm,
    rv_hbm,
    fac_hbm,
    sum_hbm,
    pool_hbm,
    out_ref,
    q_ref,
    sel_ref,
    own_ref,
    fine_ref,
    coarse,
    basis_in,
    recent_keys,
    recent_values,
    fac,
    summary,
    values,
    basis,
    centers,
    live,
    scores,
    land,
    wbuf,
    onehot,
    outgoing,
    own_w,
    theirs,
    other_out,
    bodies,
    stats,
    f_sem,
    i_sem,
    v_sem,
    pair_sem,
    send_sem,
    recv_sem,
):
    seq_pos = lax.axis_index("seq")
    core = lax.axis_index("pool")
    rows = q_ref.shape[1] // HD
    gqa = rows // heads
    pairs = heads // 2
    width = heads * HD
    tokens = fac.shape[1]
    pages = tokens // PAGE
    chunks = pages // LANES
    span = LANES * PAGE
    groups = tokens // LANES
    rank_dim = fac.shape[0]
    parts = values.shape[0] // span
    limit = len_ref[0] - seq_pos * tokens
    scale = HD ** (-0.5) * math.log2(math.e)
    partner = {"pool": 1 - core}

    def fac_load(n):
        at = pl.ds(n * span, span)
        return pltpu.make_async_copy(fac_hbm.at[:, at], fac.at[:, at], f_sem.at[n])

    def load(src, dst, n):
        copy = pltpu.make_async_copy(src, dst, i_sem.at[n])
        copy.start()
        return copy

    fac_loads = [fac_load(n) for n in range(chunks)]
    fac_loads[0].start()
    first_loads = [
        load(src, dst, n)
        for n, (src, dst) in enumerate(
            (
                (basis_hbm, basis_in),
                (sel_hbm, sel_ref),
                (q_hbm, q_ref),
                (own_hbm, own_ref),
                (fine_hbm, fine_ref),
                (coarse_hbm.at[seq_pos], coarse),
            )
        )
    ]
    for n in range(1, chunks):
        fac_loads[n].start()
    rk_load = load(rk_hbm, recent_keys, 6)
    rv_load = load(rv_hbm, recent_values, 7)
    sum_load = pltpu.make_async_copy(sum_hbm, summary, i_sem.at[8])
    loads = []
    for g in range(parts):
        at = pl.ds(g * span, span)
        loads.append(pltpu.make_async_copy(pool_hbm.at[at, :], values.at[at, :], v_sem.at[g]))

    barrier = pltpu.get_barrier_semaphore()
    for k in range(seq_count):
        peer = lax.rem(seq_pos + k, seq_count)
        for pool in (core, 1 - core)[k == 0 :]:
            pl.semaphore_signal(
                barrier,
                inc=1,
                device_id={"seq": peer, "pool": pool},
                device_id_type=MESH,
            )

    for copy in first_loads:
        copy.wait()
    low_half = iota((1, LANES), 1) < HALF
    q_flat = q_ref[...].astype(F32)
    q_rows = jnp.concatenate([q_flat[:, r * HD : (r + 1) * HD] for r in range(rows)], axis=0)
    q_swap = half_swap(q_rows)
    q_pairs = []
    q_plain = []
    for p in range(pairs):
        first = slice(2 * p * gqa, (2 * p + 1) * gqa)
        second = slice((2 * p + 1) * gqa, (2 * p + 2) * gqa)
        x = jnp.concatenate(
            [jnp.where(low_half, q_rows[first], 0.0), jnp.where(low_half, 0.0, q_swap[second])], axis=0
        )
        y = jnp.concatenate(
            [jnp.where(low_half, q_swap[first], 0.0), jnp.where(low_half, 0.0, q_rows[second])], axis=0
        )
        q_pairs.append(jnp.concatenate([x, y], axis=1).astype(BF))
        zero = jnp.zeros((gqa, HD), F32)
        plain = [
            jnp.concatenate([q_rows[first], zero], axis=1),
            jnp.concatenate([zero, q_rows[second]], axis=1),
        ]
        q_plain.append(jnp.concatenate(plain, axis=0).astype(BF))

    sel = jnp.where(core == 0, sel_ref[:heads, :], sel_ref[heads:, :]) - seq_pos * pages
    count = sel.shape[1]
    page_tok = iota((1, pages), 1) * PAGE
    spread_tok = (iota((groups, LANES), 0) * SIXTEEN + iota((groups, LANES), 1) % SIXTEEN) * PAGE
    chosen_rows = []
    for h in range(heads):
        ids = sel[h : h + 1, :]
        hi = jnp.floor_divide(ids, SIXTEEN)
        lo = ids - hi * SIXTEEN
        hit = nt(
            ones_where(iota((groups, count), 0) == hi),
            ones_where(iota((LANES, count), 0) % SIXTEEN == lo),
        )
        live[h] = jnp.where(hit > 0.5, limit - spread_tok, 0)
        by_page = jnp.concatenate([hit[g : g + 1, :SIXTEEN] for g in range(groups)], axis=1)
        chosen_rows.append(jnp.broadcast_to(by_page > 0.5, (gqa, pages)))

    chosen = [jnp.concatenate(chosen_rows[2 * p : 2 * p + 2], axis=0) for p in range(pairs)]
    owners = own_ref[...]
    before = nn(
        ones_where(owners == 1), ones_where(iota((LANES, LANES), 0) < iota((LANES, LANES), 1))
    )
    chunk_total = jnp.sum(owners.astype(F32), axis=1, keepdims=True)
    running = jnp.zeros((1, 1), F32)
    slots = []
    for c in range(chunks):
        ones = before[c : c + 1, :] + running
        running = running + chunk_total[c : c + 1, :]
        page = (iota((1, LANES), 1) + c * LANES).astype(F32)
        slots.append(jnp.where(owners[c : c + 1, :] == 1, ones + pages // 2, page - ones))
    slot = jnp.concatenate(slots, axis=1).astype(jnp.int32)
    slot = slot - (1 - core) * (pages // 2)
    slot = jnp.where(slot < 0, slot + pages, slot)
    place = slot % LANES
    column = slot - place + place % 16 * PAGE + place // 16
    column_t = jnp.swapaxes(
        jnp.concatenate([column[:, c * LANES : (c + 1) * LANES] for c in range(chunks)], axis=0).astype(
            F32
        ),
        0,
        1,
    ).astype(jnp.int32)

    for p in range(pairs):
        a = basis_in[:, 2 * p * HD : (2 * p + 1) * HD].astype(F32)
        b = basis_in[:, (2 * p + 1) * HD : (2 * p + 2) * HD].astype(F32)
        basis[:, 2 * p * HD : (2 * p + 1) * HD] = jnp.where(low_half, a, half_swap(b)).astype(BF)
        basis[:, (2 * p + 1) * HD : (2 * p + 2) * HD] = jnp.where(low_half, half_swap(a), b).astype(BF)

    lane = iota((1, LANES), 1)
    source = iota((rank_dim, LANES), 1)
    slot_of = source // SIXTEEN
    source = source % SIXTEEN * PAGE + jnp.where(
        slot_of % 2 == 0, PAGE // 2 - 1 - slot_of // 2, PAGE // 2 + slot_of // 2
    )
    page_row = iota((SIXTEEN, LANES), 0)
    lane_slot = lane // SIXTEEN
    lane_token = jnp.where(
        lane_slot % 2 == 0, PAGE // 2 - 1 - lane_slot // 2, PAGE // 2 + lane_slot // 2
    )

    def ordered(at, n):
        block = [
            jnp.take_along_axis(fac[:, at + k * LANES : at + (k + 1) * LANES].astype(F32), source, axis=1)
            for k in range(n)
        ]
        return tn(jnp.concatenate(block, axis=1).astype(BF), basis[...])

    def rotated(u, cj, sj, at):
        cm = fine_ref[at : at + SIXTEEN, :]
        sm = fine_ref[GROUP + at : GROUP + at + SIXTEEN, :]
        ca = cj * cm - sj * sm
        sa = sj * cm + cj * sm
        tiles = []
        for k in range(PAGE // 2):
            row = 2 * GROUP + k
            cb = fine_ref[row : row + 1, :]
            sb = fine_ref[row + PAGE // 2 : row + PAGE // 2 + 1, :]
            cc, ss, sc, cs = ca * cb, sa * sb, sa * cb, ca * sb
            for e, cosine, sine in ((0, cc + ss, sc - cs), (1, cc - ss, sc + cs)):
                rows_of = slice((2 * k + e) * SIXTEEN, (2 * k + e + 1) * SIXTEEN)
                cols = []
                for p in range(pairs):
                    x = u[rows_of, 2 * p * HD : (2 * p + 1) * HD]
                    y = u[rows_of, (2 * p + 1) * HD : (2 * p + 2) * HD]
                    cols.append((x * cosine - y * sine).astype(BF))
                    cols.append((y * cosine + x * sine).astype(BF))
                tiles.append(cols)
        return tiles

    def swap_bits(tiles, bits):
        tiles = list(tiles)
        for step, bit in enumerate(bits):
            clear = lane // bit % 2 == 0
            for i in range(PAGE):
                other = i | 1 << step
                if other != i:
                    a, c = tiles[i], tiles[other]
                    tiles[i] = jnp.where(clear, a, pltpu.roll(c, bit, axis=1))
                    tiles[other] = jnp.where(clear, pltpu.roll(a, LANES - bit, axis=1), c)
        return tiles

    def chunk(n, tops, u_next):
        tops = list(tops)
        by_group = [[] for _ in range(pairs)]
        for b in range(span // FINE):
            u = u_next
            j = n * (span // FINE) + b
            u_next = ordered((j + 1) * FINE, FINE // LANES) if (j + 1) * FINE < tokens else None
            cj, sj = coarse[0, j : j + 1, :], coarse[1, j : j + 1, :]
            blocks = [[] for _ in range(pairs)]
            for e in range(FINE // LANES):
                tiles = rotated(u[e * LANES : (e + 1) * LANES, :], cj, sj, e * SIXTEEN)
                g = (n * (span // FINE) + b) * (FINE // LANES) + e
                used = jnp.clip(limit - (g * SIXTEEN + page_row) * PAGE, 0, PAGE).astype(F32).astype(BF)
                for c in range(heads):
                    always = tiles[ORDER.index(0)][c]
                    column_tiles = [
                        t[c] if i == 0 else jnp.where(used > i, t[c], always)
                        for t, i in zip(tiles, ORDER)
                    ]
                    low = functools.reduce(jnp.minimum, column_tiles)
                    high = functools.reduce(jnp.maximum, column_tiles)
                    centers[g * SIXTEEN : (g + 1) * SIXTEEN, c * HD : (c + 1) * HD] = low + high
                for p in range(pairs):
                    blocks[p] += [
                        jnp.concatenate([t[2 * p], t[2 * p + 1]], axis=1) for t in tiles
                    ]
            for p in range(pairs):
                s = nt(q_pairs[p], jnp.concatenate(blocks[p], axis=0)) * scale
                for e in range(FINE // LANES):
                    g = (n * (span // FINE) + b) * (FINE // LANES) + e
                    left = jnp.concatenate(
                        [
                            jnp.broadcast_to(live[h, g : g + 1, :], (gqa, LANES))
                            for h in (2 * p, 2 * p + 1)
                        ],
                        axis=0,
                    )
                    one = jnp.where(
                        left > lane_token, s[:, e * LANES : (e + 1) * LANES], -jnp.inf
                    )
                    tops[p] = jnp.maximum(tops[p], one)
                    by_group[p].append(one)
        for p in range(pairs):
            mine = slice(p * 2 * gqa, (p + 1) * 2 * gqa)
            by_token = swap_bits(by_group[p], (16, 32, 64))
            for i in range(PAGE):
                scores[n, mine, i * LANES : (i + 1) * LANES] = by_token[i]
        return tops, u_next

    tops = [jnp.full((2 * gqa, LANES), -1e30, F32)] * pairs
    for copy in fac_loads[:-1]:
        copy.wait()
    for copy in [sum_load] + loads:
        copy.start()
    fac_loads[-1].wait()
    u_next = ordered(0, FINE // LANES)
    for n in range(chunks):
        tops, u_next = chunk(n, tops, u_next)

    for n in range(chunks):
        wanted = jnp.broadcast_to(column_t[:, n : n + 1], (LANES, LANES))
        for t in range(chunks):
            onehot[n * LANES : (n + 1) * LANES, t * LANES : (t + 1) * LANES] = ones_where(
                wanted == iota((1, LANES), 1) + t * LANES
            )

    rk_load.wait()
    peaks = []
    recents = []
    for p in range(pairs):
        mine = slice(p * 2 * gqa, (p + 1) * 2 * gqa)
        cols = slice(p * 2 * HD, (p + 1) * 2 * HD)
        s = nt(q_pairs[p], centers[:, cols]) * (scale * 0.5)
        s = jnp.where((page_tok < limit) & jnp.logical_not(chosen[p]), s, -jnp.inf)
        land[mine, :] = s
        recent = nt(q_plain[p], recent_keys[:, cols]) * scale
        first = jnp.zeros(recent.shape, jnp.int32) + seq_pos
        recent = jnp.where(first == 0, recent, -jnp.inf)
        recents.append(recent)
        best = jnp.maximum(jnp.max(tops[p], axis=1, keepdims=True), jnp.max(s, axis=1, keepdims=True))
        peaks.append(jnp.maximum(best, jnp.max(recent, axis=1, keepdims=True)))

    totals = [jnp.zeros((2 * gqa, LANES), F32)] * pairs
    for n in range(chunks):
        for p in range(pairs):
            mine = slice(p * 2 * gqa, (p + 1) * 2 * gqa)
            for i in range(PAGE):
                w = jnp.exp2(scores[n, mine, i * LANES : (i + 1) * LANES] - peaks[p])
                totals[p] = totals[p] + w
                row = i * rows + p * 2 * gqa
                wbuf[row : row + 2 * gqa, n * LANES : (n + 1) * LANES] = w.astype(BF)

    def regroup(moved, ref):
        for t in range(pages // 2 // LANES):
            for b in range(rows // 16):
                by_token = [None] * PAGE
                for place_of, i in enumerate(ORDER):
                    row = place_of * rows + b * SIXTEEN
                    by_token[i] = moved[row : row + SIXTEEN, t * LANES : (t + 1) * LANES].astype(BF)
                by_lane = swap_bits(by_token, (1, 2, 4))
                for i in range(PAGE):
                    at = t * span + i * LANES
                    ref[b * SIXTEEN : (b + 1) * SIXTEEN, at : at + LANES] = by_lane[i]

    regroup(nn(wbuf[...], onehot[:, 0 : pages // 2]), outgoing)

    def copy_to(src, dst, sems, device):
        copy = pltpu.make_async_remote_copy(
            src_ref=src,
            dst_ref=dst,
            send_sem=sems[0],
            recv_sem=sems[1],
            device_id=device,
            device_id_type=MESH,
        )
        copy.start()
        return copy

    def spread(src, dst, n, pool, begin):
        return [
            copy_to(
                src,
                dst,
                (send_sem.at[n, k], recv_sem.at[n, k]),
                {"seq": lax.rem(seq_pos + k, seq_count), "pool": pool},
            )
            for k in range(begin, seq_count)
        ]

    pl.semaphore_wait(barrier, 2 * seq_count - 1)
    swap = copy_to(outgoing, theirs, (pair_sem.at[0], pair_sem.at[1]), partner)
    regroup(nn(wbuf[...], onehot[:, pages // 2 : pages]), own_w)

    at_lane = iota((rows, LANES), 0) == iota((rows, LANES), 1)
    land_w = []
    recent_w = []
    sums = []
    for p in range(pairs):
        mine = slice(p * 2 * gqa, (p + 1) * 2 * gqa)
        w = jnp.exp2(land[mine, :] - peaks[p])
        r = jnp.exp2(recents[p] - peaks[p])
        sums.append(
            jnp.sum(w, axis=1, keepdims=True)
            + jnp.sum(totals[p], axis=1, keepdims=True)
            + jnp.sum(r, axis=1, keepdims=True)
        )
        land_w.append(w.astype(BF))
        recent_w.append(r.astype(BF))
    as_rows = [
        jnp.sum(
            jnp.where(at_lane, jnp.concatenate(col_of, axis=0), 0.0), axis=0, keepdims=True
        )
        for col_of in (peaks, sums)
    ]
    stats[seq_pos] = jnp.concatenate(as_rows + [jnp.zeros((6, LANES), F32)], axis=0)
    stat_sends = spread(stats.at[seq_pos], stats.at[seq_pos], 0, core, 1)

    def diagonal(blocks):
        return jnp.concatenate(
            [
                blocks[h // 2][h % 2 * gqa : (h % 2 + 1) * gqa, h % 2 * HD : (h % 2 + 1) * HD]
                for h in range(heads)
            ],
            axis=0,
        )

    def weighted(ref, p, g, first):
        cols = pl.ds(pl.multiple_of(first + p * 2 * HD, 2 * HD), 2 * HD)
        return nn(
            ref[p * 2 * gqa : (p + 1) * 2 * gqa, g * span : (g + 1) * span],
            values[g * span : (g + 1) * span, cols],
        )

    rv_load.wait()
    sum_load.wait()
    mine = []
    for p in range(pairs):
        cols = slice(p * 2 * HD, (p + 1) * 2 * HD)
        mine.append(nn(land_w[p], summary[:, cols]) + nn(recent_w[p], recent_values[:, cols]))
    for g in range(parts):
        loads[g].wait()
        for p in range(pairs):
            mine[p] = mine[p] + weighted(own_w, p, g, core * width)
    bodies[core, seq_pos] = diagonal(mine).astype(BF)
    sends = spread(bodies.at[core, seq_pos], bodies.at[core, seq_pos], 1, core, 1)
    swap.wait()
    other = [jnp.zeros((2 * gqa, 2 * HD), F32)] * pairs
    for g in range(parts):
        for p in range(pairs):
            other[p] = other[p] + weighted(theirs, p, g, (1 - core) * width)
    other_out[...] = diagonal(other).astype(BF)
    sends = sends + spread(other_out, bodies.at[core, seq_pos], 2, 1 - core, 0)

    for send in stat_sends:
        send.wait()
    peak_rows = [stats[k, 0:1, :] for k in range(seq_count)]
    joint = functools.reduce(jnp.maximum, peak_rows)

    def column_of(row):
        return jnp.sum(jnp.where(at_lane, row, 0.0), axis=1, keepdims=True)

    weight_sum = jnp.zeros((1, LANES), F32)
    factors = []
    for k in range(seq_count):
        factor = jnp.exp2(peak_rows[k] - joint)
        weight_sum = weight_sum + stats[k, 1:2, :] * factor
        factors.append(factor)
    inverse = 1.0 / weight_sum
    factors = [column_of(factor * inverse) for factor in factors]
    for send in sends:
        send.wait()
    result = jnp.zeros((rows, LANES), F32)
    for k in range(seq_count):
        result = result + (bodies[0, k].astype(F32) + bodies[1, k].astype(F32)) * factors[k]
    out_ref[...] = jnp.concatenate([result[r : r + 1, :] for r in range(rows)], axis=1).astype(BF)


def local(
    seq_count,
    factors,
    basis,
    value_pool,
    page_summary,
    recent_keys,
    recent_values,
    query,
    selected,
    owner_map,
    lengths,
):
    tokens, rank_dim = factors.shape[1:]
    width = basis.shape[2]
    heads = width // HD
    rows = query.shape[1] // HD
    pages = tokens // PAGE
    chunks = pages // LANES
    span = LANES * PAGE
    parts = value_pool.shape[1] // span
    coarse, fine = [jnp.asarray(t) for t in angle_tables(tokens * seq_count, seq_count)]
    vmem = pl.BlockSpec(memory_space=pltpu.VMEM)
    hbm = pl.BlockSpec(memory_space=pl.ANY)
    dma = pltpu.SemaphoreType.DMA
    return pl.pallas_call(
        functools.partial(attention_kernel, heads, seq_count),
        out_shape=jax.ShapeDtypeStruct((1, rows * HD), BF),
        in_specs=[pl.BlockSpec(memory_space=pltpu.SMEM)] + [hbm] * 11,
        out_specs=vmem,
        scratch_shapes=[
            pltpu.VMEM(query.shape, BF),
            pltpu.VMEM(selected.shape[1:], jnp.int32),
            pltpu.VMEM((chunks, LANES), jnp.int32),
            pltpu.VMEM(fine.shape, F32),
            pltpu.VMEM(coarse.shape[1:], F32),
            pltpu.VMEM((rank_dim, width), BF),
            pltpu.VMEM((WIN, width), BF),
            pltpu.VMEM((WIN, width), BF),
            pltpu.VMEM((rank_dim, tokens), BF),
            pltpu.VMEM((pages, width), BF),
            pltpu.VMEM(value_pool.shape[1:], BF),
            pltpu.VMEM((rank_dim, width), BF),
            pltpu.VMEM((pages, width), BF),
            pltpu.VMEM((heads, tokens // LANES, LANES), jnp.int32),
            pltpu.VMEM((chunks, rows, span), F32),
            pltpu.VMEM((rows, pages), F32),
            pltpu.VMEM((PAGE * rows, pages), BF),
            pltpu.VMEM((pages, pages), BF),
            pltpu.VMEM((rows, parts * span), BF),
            pltpu.VMEM((rows, parts * span), BF),
            pltpu.VMEM((rows, parts * span), BF),
            pltpu.VMEM((rows, LANES), BF),
            pltpu.VMEM((2, seq_count, rows, LANES), BF),
            pltpu.VMEM((seq_count, 8, LANES), F32),
            dma((chunks,)),
            dma((9,)),
            dma((parts,)),
            dma((2,)),
            dma((3, seq_count)),
            dma((3, seq_count)),
        ],
        compiler_params=pltpu.CompilerParams(
            collective_id=0, has_side_effects=True, vmem_limit_bytes=60 * 1024 * 1024
        ),
    )(
        lengths,
        query,
        selected[0],
        owner_map.reshape(chunks, LANES),
        fine,
        coarse,
        basis[0],
        recent_keys[0],
        recent_values[0],
        jnp.swapaxes(factors[0], 0, 1),
        page_summary[0],
        value_pool[0],
    )


def solution(mesh):
    placed = (
        P("grp", "seq", None),
        P("grp", None, "pool"),
        P("grp", ("seq", "pool"), None),
        P("grp", "seq", "pool"),
        P("grp", None, "pool"),
        P("grp", None, "pool"),
        P("grp", "pool"),
        P("grp", None, None),
        P("grp", "seq"),
        P("grp"),
    )
    return jax.shard_map(
        functools.partial(local, mesh.shape["seq"]),
        mesh=mesh,
        in_specs=placed,
        out_specs=P("grp", "pool"),
        check_vma=False,
    )
```
